32 devices in a mesh: ctx: 8 (over z, x), head: 4 (over y, core).
Axes of the slice: x: 2, y: 2, z: 4, core: 2. Of those that a mesh axis runs over, the one named last changes fastest.
Arguments:
- attn_query: bfloat16 [4096, 6144], P('ctx', 'head'), may hold values from -16 to 16
- attn_key: bfloat16 [4096, 6144], P('ctx', 'head'), may hold values from -16 to 16
- attn_value: bfloat16 [4096, 6144], P('ctx', 'head'), may hold values from -120 to 120
- delta_query: bfloat16 [4096, 6144], P('ctx', 'head'), may hold values from -6 to 6
- delta_key: bfloat16 [4096, 6144], P('ctx', 'head'), may hold values from -6 to 6
- delta_value: bfloat16 [4096, 6144], P('ctx', 'head'), may hold values from -120 to 120
- delta_gate: float32 [4096, 48], P('ctx', 'head'), may hold values from 0.5 to 1
- delta_beta: float32 [4096, 48], P('ctx', 'head'), may hold values from 0 to 0.6, as said below
- attn_gain: float32 [6144], P('head'), may hold values from 0.1 to 1.9
- delta_gain: float32 [6144], P('head'), may hold values from 0.1 to 1.9
Outputs:
- mixed: bfloat16 [4096, 6144], P('ctx', 'head')
The draws below stay inside these ranges and needn't reach their ends.
Inputs may be any that keep to these rules, and one draw needn't show every extreme that they name: `delta_beta`: Positive.
All inputs are finite; a program needn't handle non-finite values.
Results may differ from the reference program's by a relative error of at most 0.004.
Values may be sent and summed in bfloat16 or wider, within the bound.
A program may use at most 192 MiB of HBM per device.

```python
import math
import jax
import jax.numpy as jnp
from jax import lax

HEAD_COUNT = 48
DH = 128
WIDTH = 6144
WINDOW = 1024
GROUP = 64
TOK_DEV = 512
TOKEN_COUNT = 4096


def drawn_pair(key):
    sequence_lanes = jax.random.split(jax.random.fold_in(key, 101), 2)
    queries = jnp.clip(jax.random.normal(sequence_lanes[0], (TOKEN_COUNT, HEAD_COUNT, DH), jnp.float32), -5.0, 5.0)
    keyvecs = jnp.clip(jax.random.normal(sequence_lanes[1], (TOKEN_COUNT, HEAD_COUNT, DH), jnp.float32), -5.0, 5.0)
    return (queries.reshape(TOKEN_COUNT, HEAD_COUNT * DH), keyvecs.reshape(TOKEN_COUNT, HEAD_COUNT * DH))


def scaled_values(key, salt):
    sequence_lanes = jax.random.split(jax.random.fold_in(key, salt), 1)
    values = jnp.clip(jax.random.normal(sequence_lanes[0], (TOKEN_COUNT, HEAD_COUNT, DH), jnp.float32), -4.0, 4.0)
    head_ramp = jnp.exp(math.log(3.0) * jnp.arange(HEAD_COUNT, dtype=jnp.float32) / max(HEAD_COUNT - 1, 1))
    values = values * head_ramp[None, :, None]
    return values.reshape(TOKEN_COUNT, HEAD_COUNT * DH)


def fast_heads(key):
    fraction = 0.5
    return jax.random.bernoulli(jax.random.fold_in(key, 202), fraction, (HEAD_COUNT,))


def draw_attn_query(key, part):
    return drawn_pair(key)[0].astype(jnp.bfloat16)


def draw_attn_key(key, part):
    return drawn_pair(key)[1].astype(jnp.bfloat16)


def draw_attn_value(key, part):
    return scaled_values(key, 303).astype(jnp.bfloat16)


def draw_delta_value(key, part):
    return scaled_values(key, 404).astype(jnp.bfloat16)


def draw_delta_key(key, part):
    rapid_heads = fast_heads(key)
    sequence_lanes = jax.random.split(jax.random.fold_in(key, 707), 3)
    sub_dims = max(DH * 3 // 16, 2)
    shard_count = TOKEN_COUNT // TOK_DEV
    background = jax.random.normal(sequence_lanes[0], (shard_count, TOK_DEV, HEAD_COUNT, DH), jnp.float32)
    directions = jax.random.normal(sequence_lanes[1], (shard_count, HEAD_COUNT, sub_dims, DH), jnp.float32) / math.sqrt(DH)
    loadings = jax.random.normal(sequence_lanes[2], (shard_count, TOK_DEV, HEAD_COUNT, sub_dims), jnp.float32)
    focused = 4.0 * jnp.einsum('bths,bhsd->bthd', loadings, directions)
    keyvecs = background + jnp.where(rapid_heads[None, None, :, None], 0.0, focused)
    keyvecs = jnp.clip(keyvecs, -6.0, 6.0)
    return keyvecs.reshape(TOKEN_COUNT, HEAD_COUNT * DH).astype(jnp.bfloat16)


def draw_delta_gate(key, part):
    rapid_heads = fast_heads(key)
    sequence_lanes = jax.random.split(jax.random.fold_in(key, 505), 3)
    roughness = jnp.exp(jax.random.uniform(sequence_lanes[0], (TOKEN_COUNT, HEAD_COUNT), jnp.float32, math.log(0.5), math.log(2.0)))
    log_decay_rates = jnp.where(rapid_heads[None, :], 1.0 / 40.0, 0.5 / TOKEN_COUNT) * roughness
    token_groups = jax.random.bernoulli(sequence_lanes[1], 2.0 / TOKEN_COUNT, (TOKEN_COUNT, HEAD_COUNT)) & jnp.logical_not(rapid_heads)[None, :]
    removed_entries = jax.random.uniform(sequence_lanes[2], (TOKEN_COUNT, HEAD_COUNT), jnp.float32, 0.5, 0.8)
    return jnp.where(token_groups, removed_entries, jnp.exp(-log_decay_rates)).astype(jnp.float32)


def draw_delta_beta(key, part):
    rapid_heads = fast_heads(key)
    roughness = jnp.exp(jax.random.uniform(jax.random.fold_in(key, 606), (TOKEN_COUNT, HEAD_COUNT), jnp.float32, math.log(0.5), math.log(2.0)))
    baseline = jnp.where(rapid_heads[None, :], 0.25, float(DH) / TOKEN_COUNT)
    return jnp.minimum(baseline * roughness, 0.6).astype(jnp.float32)


def steps_of(own_key, extent, cuts, low, high):
    gain = 1.0
    for dim, shards_of in cuts:
        steps = jax.random.uniform(jax.random.fold_in(jax.random.fold_in(own_key, 6), dim), (shards_of,), jnp.float32, low / len(cuts), high / len(cuts))
        gain = gain * jnp.repeat(jnp.exp(steps), extent[dim] // shards_of).reshape((-1,) + (1,) * (len(extent) - 1 - dim))
    return gain


def normal_values(rng, shape, scale, limit, cuts=(), held_as=jnp.bfloat16):
    gain = steps_of(rng, shape, cuts, -0.22, 0.18) if cuts else 1.0
    values = jax.random.normal(rng, shape, jnp.float32) * scale * gain
    return jnp.minimum(jnp.maximum(values, -limit), limit).astype(held_as)


def setup_inputs(seed: int = 0) -> dict:
    keys = jax.random.split(jax.random.key(seed), 11)
    return {
        "attn_query": draw_attn_query(jax.random.fold_in(keys[10], 71), 0),
        "attn_key": draw_attn_key(jax.random.fold_in(keys[10], 71), 0),
        "attn_value": draw_attn_value(jax.random.fold_in(keys[10], 71), 0),
        "delta_query": normal_values(keys[3], (TOKEN_COUNT, WIDTH), 1.0, 6.0, ((0, 8), (1, 4))),
        "delta_key": draw_delta_key(jax.random.fold_in(keys[10], 71), 0),
        "delta_value": draw_delta_value(jax.random.fold_in(keys[10], 71), 0),
        "delta_gate": draw_delta_gate(jax.random.fold_in(keys[10], 71), 0),
        "delta_beta": draw_delta_beta(jax.random.fold_in(keys[10], 71), 0),
        "attn_gain": jnp.clip(1.0 + 0.18 * jax.random.normal(keys[8], (WIDTH,), jnp.float32), 0.1, 1.9),
        "delta_gain": jnp.clip(1.0 + 0.18 * jax.random.normal(keys[9], (WIDTH,), jnp.float32), 0.1, 1.9),
    }


epsilon = 1e-06
highest = lax.Precision.HIGHEST

def unit_rows(values):
    return values * lax.rsqrt(lax.optimization_barrier(jnp.mean(values * values, axis=-1, keepdims=True)) + epsilon) / math.sqrt(values.shape[-1])

def group_terms(inputs):
    queries, keyvecs, values, alphas, betas = inputs
    length = alphas.shape[0]
    log_sums = jnp.cumsum(jnp.log(alphas), axis=0)
    causal = jnp.arange(length, dtype=jnp.int32)[:, None] >= jnp.arange(length, dtype=jnp.int32)[None, :]
    spread = log_sums.T[:, :, None] - log_sums.T[:, None, :]
    ratios = jnp.exp(jnp.where(causal[None], spread, -1e+30))
    identity = jnp.eye(length, dtype=jnp.float32)
    key_gram = jnp.einsum('rhd,shd->hrs', keyvecs, keyvecs, precision=highest)
    negated = -(betas.T[:, :, None] * ratios * (1.0 - identity) * key_gram)
    inverse = identity + negated
    powered = negated
    for doubling in range(max((length - 1).bit_length() - 1, 0)):
        powered = jnp.einsum('hij,hjk->hik', powered, powered, precision=highest)
        inverse = inverse + jnp.einsum('hij,hjk->hik', inverse, powered, precision=highest)
    growth = jnp.exp(log_sums)
    scaled_vals = jnp.transpose(betas[:, :, None] * values, (1, 0, 2))
    scaled_keys = jnp.transpose((betas * growth)[:, :, None] * keyvecs, (1, 0, 2))
    pseudo_vals = jnp.einsum('hij,hjd->hid', inverse, scaled_vals, precision=highest)
    pseudo_keys = jnp.einsum('hij,hjd->hid', inverse, scaled_keys, precision=highest)
    decay_tail = jnp.exp(log_sums[-1][:, None] - log_sums.T)
    return (log_sums, ratios, growth, decay_tail, pseudo_vals, pseudo_keys)

def group_step(current, inputs):
    queries, keyvecs, values, alphas, betas = inputs
    log_sums, ratios, growth, decay_tail, pseudo_vals, pseudo_keys = group_terms(inputs)
    errors = pseudo_vals - jnp.einsum('hcd,hde->hce', pseudo_keys, current, precision=highest)
    mixing = jnp.einsum('rhd,shd->hrs', queries, keyvecs, precision=highest) * ratios
    outputs = growth.T[:, :, None] * jnp.einsum('chd,hde->hce', queries, current, precision=highest)
    outputs = outputs + jnp.einsum('hrs,hse->hre', mixing, errors, precision=highest)
    new_state = jnp.exp(log_sums[-1])[:, None, None] * current
    new_state = new_state + jnp.einsum('chd,hc,hce->hde', keyvecs, decay_tail, errors, precision=highest)
    return (new_state, jnp.transpose(outputs, (1, 0, 2)))

def delta_inputs(queries, keyvecs, values, alphas, betas):
    length = alphas.shape[0]
    count = alphas.shape[1]
    blocks = length // GROUP

    def to_blocks(array):
        return array.astype(jnp.float32).reshape(blocks, GROUP, count, DH)
    return (unit_rows(to_blocks(queries)), unit_rows(to_blocks(keyvecs)), to_blocks(values), alphas.reshape(blocks, GROUP, count), betas.reshape(blocks, GROUP, count))

def attend(queries, keyvecs, values, query_start, key_start):
    scores = jnp.einsum('qhd,khd->hqk', queries.astype(jnp.float32), keyvecs.astype(jnp.float32)) / math.sqrt(queries.shape[-1])
    query_pos = query_start + jnp.arange(queries.shape[0], dtype=jnp.int32)[:, None]
    key_pos = key_start + jnp.arange(keyvecs.shape[0], dtype=jnp.int32)[None, :]
    distance = query_pos - key_pos
    allowed = (distance >= 0) & (distance < WINDOW) & (key_pos >= 0)
    scores = jnp.where(allowed[None], scores, -1e+30)
    maxima = lax.optimization_barrier(jnp.max(scores, axis=-1, keepdims=True))
    raised = jnp.exp(scores - maxima)
    weights = (raised / lax.optimization_barrier(jnp.sum(raised, axis=-1, keepdims=True))).astype(jnp.bfloat16)
    return jnp.einsum('hqk,khd->qhd', weights.astype(jnp.float32), values.astype(jnp.float32))

def window_attention(queries, keyvecs, values):
    length = queries.shape[0]
    block_rows = math.gcd(length, 512)
    padded_keys = jnp.concatenate([jnp.zeros((WINDOW, WIDTH), jnp.bfloat16), keyvecs], axis=0)
    padded_vals = jnp.concatenate([jnp.zeros((WINDOW, WIDTH), jnp.bfloat16), values], axis=0)

    def one_block(start):
        query_blk = lax.dynamic_slice_in_dim(queries, start, block_rows, 0).reshape(block_rows, HEAD_COUNT, DH)
        key_blk = lax.dynamic_slice_in_dim(padded_keys, start, block_rows + WINDOW, 0).reshape(block_rows + WINDOW, HEAD_COUNT, DH)
        value_blk = lax.dynamic_slice_in_dim(padded_vals, start, block_rows + WINDOW, 0).reshape(block_rows + WINDOW, HEAD_COUNT, DH)
        return attend(query_blk, key_blk, value_blk, start, start - WINDOW)
    starts = jnp.arange(length // block_rows, dtype=jnp.int32) * block_rows
    outputs = lax.map(one_block, starts)
    return outputs.reshape(length, WIDTH)

def reference(attn_query, attn_key, attn_value, delta_query, delta_key, delta_value, delta_gate, delta_beta, attn_gain, delta_gain):
    attn_out = window_attention(attn_query, attn_key, attn_value)
    prepared = delta_inputs(delta_query, delta_key, delta_value, delta_gate, delta_beta)
    current = jnp.zeros((HEAD_COUNT, DH, DH), jnp.float32)
    final_state, delta_blocks = lax.scan(group_step, current, prepared)
    delta_out = delta_blocks.reshape(TOKEN_COUNT, WIDTH)
    scale_attn = lax.rsqrt(lax.optimization_barrier(jnp.mean(attn_out * attn_out, axis=-1, keepdims=True)) + epsilon)
    scale_delta = lax.rsqrt(lax.optimization_barrier(jnp.mean(delta_out * delta_out, axis=-1, keepdims=True)) + epsilon)
    joined = 0.5 * (attn_gain * attn_out * scale_attn + delta_gain * delta_out * scale_delta)
    return joined.astype(jnp.bfloat16)
```

```python
import functools
import math

import jax
import jax.numpy as jnp
from jax import lax
from jax.experimental import pallas as pl
from jax.experimental.pallas import tpu as pltpu
from jax.sharding import PartitionSpec as P

DH = 128
WINDOW = 1024
CHUNK = 128
QROWS = 256
FAR_AHEAD = 4
NEAR_AHEAD = 2
PASS_AHEAD = 1
ATTEND_LAG = 1
HOP = 1
HEADS_STEP = 2

epsilon = 1e-06
f32 = jnp.float32
bf16 = jnp.bfloat16


def dot(left, right, dims=((1,), (0,))):
    return lax.dot_general(left, right, (dims, ((), ())), preferred_element_type=f32)


def dot1(left, right, dims=((1,), (0,))):
    return dot(left.astype(bf16), right.astype(bf16), dims)


def split(value):
    high = value.astype(bf16)
    return high, (value - high.astype(f32)).astype(bf16)


def dot3(left, right, dims=((1,), (0,))):
    lh, ll = split(left)
    rh, rl = split(right)
    return dot(lh, rh, dims) + (dot(lh, rl, dims) + dot(ll, rh, dims))


def unit_scale(raw):
    wide = raw.astype(f32)
    mean = jnp.mean(wide * wide, axis=-1, keepdims=True)
    return lax.rsqrt(mean + epsilon) / math.sqrt(DH)


def delta_heads(first, q_ref, k_ref, v_ref, gate_ref, beta_ref, out_ref, qeff_ref, lin_ref, off_ref):
    rows = q_ref.shape[0]
    chunks = rows // CHUNK
    ri = lax.broadcasted_iota(jnp.int32, (CHUNK, CHUNK), 0)
    ci = lax.broadcasted_iota(jnp.int32, (CHUNK, CHUNK), 1)
    eye = ri == ci
    lower = ri >= ci
    strict = ri > ci
    identity = jnp.where(eye, 1.0, 0.0).astype(f32)

    def column(row):
        return jnp.sum(jnp.where(eye, row, 0.0), axis=1, keepdims=True)

    def as_row(col):
        return jnp.sum(jnp.where(eye, col, 0.0), axis=0, keepdims=True)

    units = [(h, c) for c in range(chunks) for h in range(HEADS_STEP)]
    terms = {}
    for h, c in units:
        rs = slice(c * CHUNK, (c + 1) * CHUNK)
        cs = pl.ds(pl.multiple_of((first + h) * DH, DH), DH)
        q, k = q_ref[rs, cs], k_ref[rs, cs]
        log_row = jnp.log(gate_ref[first + h, :, rs])
        log_col = column(log_row)
        beta_col = column(beta_ref[first + h, :, rs])
        sum_row = jnp.sum(jnp.where(ri <= ci, log_col, 0.0), axis=0, keepdims=True)
        sum_col = jnp.sum(jnp.where(lower, log_row, 0.0), axis=1, keepdims=True)
        total = jnp.sum(log_row, axis=1, keepdims=True)
        sk, sq = unit_scale(k), unit_scale(q)
        sk_row = as_row(sk)
        ratios = jnp.exp(jnp.where(lower, sum_col - sum_row, -1e30)) * sk_row
        both = dot(jnp.concatenate([k, q], axis=0), k, ((1,), (1,)))
        low = jnp.where(strict, (beta_col * sk) * ratios * both[:CHUNK], 0.0)
        mix = (sq * ratios) * both[CHUNK:]
        growth = jnp.exp(sum_col)
        terms[h, c] = dict(
            low=low,
            mix=mix.astype(bf16),
            inv=identity - jnp.where((ri // 2) == (ci // 2), low, 0.0),
            beta=beta_col,
            gk=growth * sk,
            gq=growth * sq,
            tail=jnp.exp(total - sum_col) * sk,
            last=jnp.exp(total),
        )
    size = 2
    while size < CHUNK:
        pick = ((ri // (2 * size)) == (ci // (2 * size))) & ((ri // size) != (ci // size))
        for u in units:
            t = terms[u]
            t["tmp"] = dot1(jnp.where(pick, t["low"], 0.0), t["inv"])
        for u in units:
            t = terms[u]
            t["inv"] = t["inv"] - dot1(t["inv"], t["tmp"])
        size *= 2
    states = [None] * HEADS_STEP
    for c in range(chunks):
        rs = slice(c * CHUNK, (c + 1) * CHUNK)
        for h in range(HEADS_STEP):
            cs = pl.ds(pl.multiple_of((first + h) * DH, DH), DH)
            t = terms[h, c]
            q, k, v = q_ref[rs, cs], k_ref[rs, cs], v_ref[rs, cs].astype(f32)
            zero = jnp.zeros((CHUNK, DH), f32)
            if c == 0:
                state = jnp.concatenate([jnp.zeros((DH, DH), f32), identity], axis=1)
                ks = jnp.concatenate([zero, k.astype(f32)], axis=1)
                qs = jnp.concatenate([zero, q.astype(f32)], axis=1)
            else:
                state = states[h]
                sb = state.astype(bf16)
                kqs = dot(jnp.concatenate([k, q], axis=0), sb)
                ks, qs = kqs[:CHUNK], kqs[CHUNK:]
            resid = jnp.concatenate([v, zero], axis=1) - t["gk"] * ks
            errors = dot1(t["inv"], t["beta"] * resid)
            out = t["gq"] * qs + dot(t["mix"], errors.astype(bf16))
            out_ref[first + h, rs] = out[:, :DH]
            qeff_ref[first + h, rs] = out[:, DH:].astype(bf16)
            states[h] = t["last"] * state + dot(
                k, (t["tail"] * errors).astype(bf16), ((0,), (0,))
            )
    for h in range(HEADS_STEP):
        off_ref[first + h] = states[h][:, :DH]
        lin_ref[first + h] = states[h][:, DH:]


def layer_kernel(
    aq_hbm, ak_hbm, av_hbm, dq_hbm, dk_hbm, dv_hbm, gates_hbm, betas_hbm, again_ref, dgain_ref,
    mixed_hbm,
    aq_ref, dq_ref, dk_ref, dv_ref, gates_ref, betas_ref,
    keys, vals, attn_out, delta_out, qeff, linear, offset, entering, leaving, attn_sq, delta_sq,
    sums_send, sums_recv, gate_ref, beta_ref, mixed_ref,
    out_sem, own_sem, far_send, far_recv, near_send, near_recv, relay_send, relay_recv, sums_ss, sums_rs,
    query_sem, gates_sem, delta_sem,
    *, contexts, groups,
):
    rows, width = aq_hbm.shape
    heads = width // DH
    me = lax.axis_index("ctx")
    group = lax.axis_index("head")
    odd = lax.rem(me, 2) == 1
    even = lax.rem(me, 2) == 0
    back = WINDOW
    halves = rows // QROWS
    blocks = rows // CHUNK
    steps = heads // HEADS_STEP
    units = 2 * heads

    both = ((0, ak_hbm, keys), (1, av_hbm, vals))
    far_rows = pl.ds(0, rows)
    near_rows = pl.ds(rows, rows)
    own_rows = pl.ds(back, rows)

    def lanes(h):
        return pl.ds(pl.multiple_of(h * DH, DH), DH)

    def own_copy(h, kind, source, buffer):
        return pltpu.make_async_copy(
            source.at[:, lanes(h)], buffer.at[h, own_rows], own_sem.at[kind, h]
        )

    def far_copy(h, kind, source, buffer):
        return pltpu.make_async_remote_copy(
            src_ref=source.at[:, lanes(h)],
            dst_ref=buffer.at[h, far_rows],
            send_sem=far_send.at[kind, h],
            recv_sem=far_recv.at[kind, h],
            device_id={"ctx": lax.rem(me + 2, contexts)},
            device_id_type=pl.DeviceIdType.MESH,
        )

    def near_copy(h, kind, source, buffer):
        return pltpu.make_async_remote_copy(
            src_ref=source.at[:, lanes(h)],
            dst_ref=buffer.at[h, near_rows],
            send_sem=near_send.at[kind, h],
            recv_sem=near_recv.at[kind, h],
            device_id={"ctx": lax.rem(me + 1, contexts)},
            device_id_type=pl.DeviceIdType.MESH,
        )

    def forward_copy(h, kind, source, buffer):
        return pltpu.make_async_remote_copy(
            src_ref=buffer.at[h, far_rows],
            dst_ref=buffer.at[h, near_rows],
            send_sem=near_send.at[kind, h],
            recv_sem=near_recv.at[kind, h],
            device_id={"ctx": lax.rem(me + contexts - 1, contexts)},
            device_id_type=pl.DeviceIdType.MESH,
        )

    def pair(p):
        return pl.ds(p * HEADS_STEP, HEADS_STEP)

    def relay_copy(p):
        return pltpu.make_async_remote_copy(
            src_ref=leaving.at[pair(p)],
            dst_ref=entering.at[pair(p)],
            send_sem=relay_send.at[p],
            recv_sem=relay_recv.at[p],
            device_id={"ctx": lax.rem(me + 1, contexts)},
            device_id_type=pl.DeviceIdType.MESH,
        )

    def pair_lanes(p):
        return pl.ds(pl.multiple_of(p * HEADS_STEP * DH, HEADS_STEP * DH), HEADS_STEP * DH)

    inputs = ((0, dq_hbm, dq_ref), (1, dk_hbm, dk_ref), (2, dv_hbm, dv_ref))

    def delta_load(p, kind, source, buffer):
        return pltpu.make_async_copy(
            source.at[:, pair_lanes(p)], buffer.at[:, pair_lanes(p)], delta_sem.at[kind, p]
        )

    gate_load = pltpu.make_async_copy(gates_hbm, gates_ref, gates_sem.at[0])
    beta_load = pltpu.make_async_copy(betas_hbm, betas_ref, gates_sem.at[1])
    query_load = pltpu.make_async_copy(aq_hbm, aq_ref, query_sem.at[0])

    def of_unit(u, action):
        h = u // 2
        for args in both:
            @pl.when(lax.rem(u, 2) == args[0])
            def _():
                action(h, *args)

    def send_far(u):
        @pl.when((u < units) & (me + 2 < contexts))
        def _():
            of_unit(u, lambda *args: far_copy(*args).start())

    def send_near(u):
        @pl.when((u < units) & even)
        def _():
            of_unit(u, lambda *args: near_copy(*args).start())

    def send_on(u):
        def action(*args):
            far_copy(*args).wait_recv()
            forward_copy(*args).start()

        @pl.when((u < units) & odd & (me >= 3))
        def _():
            of_unit(u, action)

    gate_load.start()
    beta_load.start()
    for args in inputs:
        delta_load(0, *args).start()

    barrier = pltpu.get_barrier_semaphore()
    for by in (-2, -1, 1, 2):
        @pl.when((me + by >= 0) & (me + by < contexts))
        def _():
            pl.semaphore_signal(
                barrier, inc=1, device_id={"ctx": me + by}, device_id_type=pl.DeviceIdType.MESH
            )
    for by in range(1, groups):
        pl.semaphore_signal(
            barrier, inc=1, device_id={"head": lax.rem(group + by, groups)},
            device_id_type=pl.DeviceIdType.MESH,
        )

    def start_delta(p, carry):
        for args in inputs:
            delta_load(p, *args).start()
        return carry

    lax.fori_loop(1, steps, start_delta, 0)

    near_peers = jnp.minimum(me, 2) + jnp.minimum(contexts - 1 - me, 2)
    pl.semaphore_wait(barrier, near_peers + (groups - 1))

    lax.fori_loop(0, FAR_AHEAD, lambda u, c: (send_far(u), c)[1], 0)
    lax.fori_loop(0, NEAR_AHEAD, lambda u, c: (send_near(u), c)[1], 0)
    query_load.start()

    def start_own(h, carry):
        for args in both:
            own_copy(h, *args).start()
        return carry

    lax.fori_loop(0, heads, start_own, 0)

    @pl.when(me < 2)
    def _():
        def clear(h, carry):
            keys[h, far_rows] = jnp.zeros((rows, DH), bf16)
            vals[h, far_rows] = jnp.zeros((rows, DH), bf16)
            return carry
        lax.fori_loop(0, heads, clear, 0)

    @pl.when(me < 1)
    def _():
        def clear(h, carry):
            keys[h, near_rows] = jnp.zeros((rows, DH), bf16)
            vals[h, near_rows] = jnp.zeros((rows, DH), bf16)
            entering[h] = jnp.zeros((DH, DH), bf16)
            return carry
        lax.fori_loop(0, heads, clear, 0)

    gate_load.wait()
    beta_load.wait()
    gate_rows, beta_rows = gates_ref[...].T, betas_ref[...].T
    for h in range(heads):
        gate_ref[h] = gate_rows[h : h + 1]
        beta_ref[h] = beta_rows[h : h + 1]
    attn_sq[...] = jnp.zeros_like(attn_sq)
    delta_sq[...] = jnp.zeros_like(delta_sq)

    scale = math.log2(math.e) / math.sqrt(DH)
    ri = lax.broadcasted_iota(jnp.int32, (QROWS, QROWS), 0)
    ci = lax.broadcasted_iota(jnp.int32, (QROWS, QROWS), 1)
    tiles = WINDOW // QROWS + 1
    first_tile = jnp.maximum(WINDOW - me * rows, 0) // QROWS

    def attend(h, b):
        q_rows = pl.ds(pl.multiple_of(b * QROWS, QROWS), QROWS)
        q = aq_ref[q_rows, lanes(h)]
        scores = []
        for n in range(tiles):
            at = pl.ds(pl.multiple_of((b + n) * QROWS, QROWS), QROWS)
            s = dot(q, keys[h, at], ((1,), (1,))) * scale
            if n < tiles - 1:
                s = s + jnp.where(b + n >= first_tile, 0.0, -1e30).astype(f32)
            if n == 0:
                s = jnp.where(ci > ri, s, -1e30)
            if n == tiles - 1:
                s = jnp.where(ci <= ri, s, -1e30)
            scores.append(s)
        top = jnp.max(functools.reduce(jnp.maximum, scores), axis=1, keepdims=True)
        raised = [jnp.exp2(s - top) for s in scores]
        total = jnp.sum(functools.reduce(jnp.add, raised), axis=1, keepdims=True)
        inverse = 1.0 / total
        out = None
        for n in range(tiles):
            at = pl.ds(pl.multiple_of((b + n) * QROWS, QROWS), QROWS)
            part = dot((raised[n] * inverse).astype(bf16), vals[h, at])
            out = part if out is None else out + part
        attn_out[h, q_rows] = out
        attn_sq[q_rows, :] += out * out

    def relay(p):
        @pl.when(me >= 1)
        def _():
            relay_copy(p).wait_recv()

        @pl.when(me + 1 < contexts)
        def _():
            for e in range(HEADS_STEP):
                h = p * HEADS_STEP + e
                high, low = split(linear[h])
                state = entering[h]
                leaving[h] = (dot(high, state) + dot(low, state) + offset[h]).astype(bf16)
            relay_copy(p).start()

        for e in range(HEADS_STEP):
            h = p * HEADS_STEP + e
            full = delta_out[h] + dot(qeff[h], entering[h])
            delta_out[h] = full
            delta_sq[...] += full * full

    def service(t):
        q = t - HOP * me

        @pl.when((q >= 0) & (lax.rem(q + 2 * contexts * HOP, 2) == 0) & (q < 2 * steps))
        def _():
            relay(q // 2)

        send_far(t + FAR_AHEAD)
        send_near(t + NEAR_AHEAD)

        @pl.when(t == 0)
        def _():
            lax.fori_loop(0, PASS_AHEAD, lambda u, c: (send_on(u), c)[1], 0)

        send_on(t + PASS_AHEAD)

    def step(s, carry):
        @pl.when(s < steps)
        def _():
            for args in inputs:
                delta_load(s, *args).wait()
            delta_heads(
                s * HEADS_STEP, dq_ref, dk_ref, dv_ref, gate_ref, beta_ref,
                delta_out, qeff, linear, offset,
            )

        service(2 * s)
        h = s - ATTEND_LAG

        @pl.when((h >= 0) & (h < heads))
        def _():
            @pl.when(h == 0)
            def _():
                query_load.wait()

            for args in both:
                own_copy(h, *args).wait()

                @pl.when((me >= 2) & jnp.logical_not(odd & (me >= 3)))
                def _():
                    far_copy(h, *args).wait_recv()

                @pl.when(me >= 1)
                def _():
                    near_copy(h, *args).wait_recv()

            attend(h, 0)

        service(2 * s + 1)

        @pl.when((h >= 0) & (h < heads))
        def _():
            lax.fori_loop(1, halves, lambda b, c: (attend(h, b), c)[1], 0)

        return carry

    turns = max(heads + ATTEND_LAG, steps + (HOP * (contexts - 1)) // 2 + 1)
    lax.fori_loop(0, turns, step, 0)

    dr = lax.broadcasted_iota(jnp.int32, (CHUNK, CHUNK), 0)
    dc = lax.broadcasted_iota(jnp.int32, (CHUNK, CHUNK), 1)
    eye = dr == dc
    lines = []
    for part in (attn_sq, delta_sq):
        for b in range(blocks):
            col = jnp.sum(part[b * CHUNK : (b + 1) * CHUNK, :], axis=1, keepdims=True)
            lines.append(jnp.sum(jnp.where(eye, col, 0.0), axis=0, keepdims=True))
    mine = jnp.concatenate(lines, axis=0)
    sums_send[...] = mine

    def sums_copy(by):
        return pltpu.make_async_remote_copy(
            src_ref=sums_send,
            dst_ref=sums_recv.at[by],
            send_sem=sums_ss.at[by],
            recv_sem=sums_rs.at[by],
            device_id={"head": lax.rem(group + by, groups)},
            device_id_type=pl.DeviceIdType.MESH,
        )

    for by in range(1, groups):
        sums_copy(by).start()
    whole = mine
    for by in range(1, groups):
        sums_copy(by).wait_recv()
        whole = whole + sums_recv[by]
    scales = lax.rsqrt(whole / (width * groups) + epsilon) * 0.5

    def out_copy(b):
        span = pl.ds(b * CHUNK, CHUNK)
        return pltpu.make_async_copy(mixed_ref.at[span], mixed_hbm.at[span], out_sem.at[b])

    for b in range(blocks):
        rs = slice(b * CHUNK, (b + 1) * CHUNK)
        sa = jnp.sum(jnp.where(eye, scales[b : b + 1], 0.0), axis=1, keepdims=True)
        sd = jnp.sum(
            jnp.where(eye, scales[blocks + b : blocks + b + 1], 0.0), axis=1, keepdims=True
        )
        for h in range(heads):
            cs = slice(h * DH, (h + 1) * DH)
            mixed_ref[rs, cs] = (
                again_ref[cs][None, :] * attn_out[h, rs] * sa + dgain_ref[cs][None, :] * delta_out[h, rs] * sd
            ).astype(bf16)
        out_copy(b).start()

    for b in range(blocks):
        out_copy(b).wait()
    for by in range(1, groups):
        sums_copy(by).wait_send()

    def drain(h, carry):
        for args in both:
            @pl.when(me + 2 < contexts)
            def _():
                far_copy(h, *args).wait_send()

            @pl.when(even)
            def _():
                near_copy(h, *args).wait_send()

            @pl.when(odd & (me >= 3))
            def _():
                forward_copy(h, *args).wait_send()

        return carry

    lax.fori_loop(0, heads, drain, 0)

    @pl.when(me + 1 < contexts)
    def _():
        lax.fori_loop(0, steps, lambda p, c: (relay_copy(p).wait_send(), c)[1], 0)


def on_device(
    attn_query,
    attn_key,
    attn_value,
    delta_query,
    delta_key,
    delta_value,
    delta_gate,
    delta_beta,
    attn_gain,
    delta_gain,
):
    rows, width = attn_query.shape
    heads = width // DH
    groups = lax.axis_size("head")
    lines = 2 * rows // CHUNK
    vmem = pl.BlockSpec(memory_space=pltpu.VMEM)
    hbm = pl.BlockSpec(memory_space=pl.ANY)
    dma = pltpu.SemaphoreType.DMA
    return pl.pallas_call(
        functools.partial(layer_kernel, contexts=lax.axis_size("ctx"), groups=groups),
        in_specs=[hbm] * 8 + [vmem] * 2,
        out_specs=hbm,
        out_shape=jax.ShapeDtypeStruct((rows, width), bf16),
        scratch_shapes=[
            pltpu.VMEM((rows, width), bf16),
            pltpu.VMEM((rows, width), bf16),
            pltpu.VMEM((rows, width), bf16),
            pltpu.VMEM((rows, width), bf16),
            pltpu.VMEM((rows, heads), f32),
            pltpu.VMEM((rows, heads), f32),
            pltpu.VMEM((heads, WINDOW + rows, DH), bf16),
            pltpu.VMEM((heads, WINDOW + rows, DH), bf16),
            pltpu.VMEM((heads, rows, DH), f32),
            pltpu.VMEM((heads, rows, DH), f32),
            pltpu.VMEM((heads, rows, DH), bf16),
            pltpu.VMEM((heads, DH, DH), f32),
            pltpu.VMEM((heads, DH, DH), f32),
            pltpu.VMEM((heads, DH, DH), bf16),
            pltpu.VMEM((heads, DH, DH), bf16),
            pltpu.VMEM((rows, DH), f32),
            pltpu.VMEM((rows, DH), f32),
            pltpu.VMEM((lines, CHUNK), f32),
            pltpu.VMEM((groups, lines, CHUNK), f32),
            pltpu.VMEM((heads, 1, rows), f32),
            pltpu.VMEM((heads, 1, rows), f32),
            pltpu.VMEM((rows, width), bf16),
            dma((rows // CHUNK,)),
            dma((2, heads)),
            dma((2, heads)),
            dma((2, heads)),
            dma((2, heads)),
            dma((2, heads)),
            dma((heads // HEADS_STEP,)),
            dma((heads // HEADS_STEP,)),
            dma((groups,)),
            dma((groups,)),
            dma((1,)),
            dma((2,)),
            dma((3, heads // HEADS_STEP)),
        ],
        compiler_params=pltpu.CompilerParams(
            collective_id=0, has_side_effects=True, vmem_limit_bytes=60 * 1024 * 1024
        ),
        name="layer",
    )(
        attn_query,
        attn_key,
        attn_value,
        delta_query,
        delta_key,
        delta_value,
        delta_gate,
        delta_beta,
        attn_gain,
        delta_gain,
    )


def solution(mesh):
    both = P("ctx", "head")
    return jax.shard_map(
        on_device,
        mesh=mesh,
        in_specs=(both,) * 8 + (P("head"),) * 2,
        out_specs=both,
        check_vma=False,
    )
```

```python
import functools
import math

import jax
import jax.numpy as jnp
from jax import lax
from jax.experimental import pallas as pl
from jax.experimental.pallas import tpu as pltpu
from jax.sharding import PartitionSpec as P

DH = 128
WINDOW = 1024
CHUNK = 128
QROWS = 256
FAR_AHEAD = 3
NEAR_AHEAD = 2
PASS_AHEAD = 1
ATTEND_LAG = 1
HOP = 1
RATE = 5
HEADS_STEP = 2

epsilon = 1e-06
f32 = jnp.float32
bf16 = jnp.bfloat16


def dot(left, right, dims=((1,), (0,))):
    return lax.dot_general(left, right, (dims, ((), ())), preferred_element_type=f32)


def dot1(left, right, dims=((1,), (0,))):
    return dot(left.astype(bf16), right.astype(bf16), dims)


def split(value):
    high = value.astype(bf16)
    return high, (value - high.astype(f32)).astype(bf16)


def dot3(left, right, dims=((1,), (0,))):
    lh, ll = split(left)
    rh, rl = split(right)
    return dot(lh, rh, dims) + (dot(lh, rl, dims) + dot(ll, rh, dims))


def unit_scale(raw):
    wide = raw.astype(f32)
    mean = jnp.mean(wide * wide, axis=-1, keepdims=True)
    return lax.rsqrt(mean + epsilon) / math.sqrt(DH)


def delta_heads(first, between, q_ref, k_ref, v_ref, gate_ref, beta_ref, out_ref, qeff_ref, lin_ref, off_ref):
    rows = q_ref.shape[0]
    chunks = rows // CHUNK
    ri = lax.broadcasted_iota(jnp.int32, (CHUNK, CHUNK), 0)
    ci = lax.broadcasted_iota(jnp.int32, (CHUNK, CHUNK), 1)
    eye = ri == ci
    lower = ri >= ci
    strict = ri > ci
    identity = jnp.where(eye, 1.0, 0.0).astype(f32)

    def column(row):
        return jnp.sum(jnp.where(eye, row, 0.0), axis=1, keepdims=True)

    def as_row(col):
        return jnp.sum(jnp.where(eye, col, 0.0), axis=0, keepdims=True)

    units = [(h, c) for c in range(chunks) for h in range(HEADS_STEP)]
    terms = {}
    for h, c in units:
        rs = slice(c * CHUNK, (c + 1) * CHUNK)
        cs = pl.ds(pl.multiple_of((first + h) * DH, DH), DH)
        q, k = q_ref[rs, cs], k_ref[rs, cs]
        log_row = jnp.log(gate_ref[first + h, :, rs])
        log_col = column(log_row)
        beta_col = column(beta_ref[first + h, :, rs])
        sum_row = jnp.sum(jnp.where(ri <= ci, log_col, 0.0), axis=0, keepdims=True)
        sum_col = jnp.sum(jnp.where(lower, log_row, 0.0), axis=1, keepdims=True)
        total = jnp.sum(log_row, axis=1, keepdims=True)
        sk, sq = unit_scale(k), unit_scale(q)
        sk_row = as_row(sk)
        ratios = jnp.exp(jnp.where(lower, sum_col - sum_row, -1e30)) * sk_row
        both = dot(jnp.concatenate([k, q], axis=0), k, ((1,), (1,)))
        low = jnp.where(strict, (beta_col * sk) * ratios * both[:CHUNK], 0.0)
        mix = (sq * ratios) * both[CHUNK:]
        growth = jnp.exp(sum_col)
        terms[h, c] = dict(
            low=low,
            mix=mix.astype(bf16),
            inv=identity - jnp.where((ri // 2) == (ci // 2), low, 0.0),
            beta=beta_col,
            gk=growth * sk,
            gq=growth * sq,
            tail=jnp.exp(total - sum_col) * sk,
            last=jnp.exp(total),
        )
    size = 2
    while size < CHUNK:
        pick = ((ri // (2 * size)) == (ci // (2 * size))) & ((ri // size) != (ci // size))
        for u in units:
            t = terms[u]
            t["tmp"] = dot1(jnp.where(pick, t["low"], 0.0), t["inv"])
        for u in units:
            t = terms[u]
            t["inv"] = t["inv"] - dot1(t["inv"], t["tmp"])
        size *= 2
    between()
    states = [None] * HEADS_STEP
    for c in range(chunks):
        rs = slice(c * CHUNK, (c + 1) * CHUNK)
        for h in range(HEADS_STEP):
            cs = pl.ds(pl.multiple_of((first + h) * DH, DH), DH)
            t = terms[h, c]
            q, k, v = q_ref[rs, cs], k_ref[rs, cs], v_ref[rs, cs].astype(f32)
            zero = jnp.zeros((CHUNK, DH), f32)
            if c == 0:
                state = jnp.concatenate([jnp.zeros((DH, DH), f32), identity], axis=1)
                ks = jnp.concatenate([zero, k.astype(f32)], axis=1)
                qs = jnp.concatenate([zero, q.astype(f32)], axis=1)
            else:
                state = states[h]
                sb = state.astype(bf16)
                kqs = dot(jnp.concatenate([k, q], axis=0), sb)
                ks, qs = kqs[:CHUNK], kqs[CHUNK:]
            resid = jnp.concatenate([v, zero], axis=1) - t["gk"] * ks
            errors = dot1(t["inv"], t["beta"] * resid)
            out = t["gq"] * qs + dot(t["mix"], errors.astype(bf16))
            out_ref[first + h, rs] = out[:, :DH]
            qeff_ref[first + h, rs] = out[:, DH:].astype(bf16)
            states[h] = t["last"] * state + dot(
                k, (t["tail"] * errors).astype(bf16), ((0,), (0,))
            )
    for h in range(HEADS_STEP):
        off_ref[first + h] = states[h][:, :DH]
        lin_ref[first + h] = states[h][:, DH:]


def layer_kernel(
    aq_hbm, ak_hbm, av_hbm, dq_hbm, dk_hbm, dv_hbm, gates_hbm, betas_hbm, again_hbm, dgain_hbm,
    mixed_ref,
    aq_ref, dq_ref, dk_ref, dv_ref, gates_ref, betas_ref,
    keys, vals, attn_out, delta_out, qeff, linear, offset, entering, leaving, attn_sq, delta_sq,
    sums_send, sums_recv, gate_ref, beta_ref, again_ref, dgain_ref,
    gain_sem, own_sem, far_send, far_recv, near_send, near_recv, relay_send, relay_recv, sums_ss, sums_rs,
    query_sem, gates_sem, delta_sem,
    *, contexts, groups,
):
    rows, width = aq_hbm.shape
    heads = width // DH
    me = lax.axis_index("ctx")
    group = lax.axis_index("head")
    odd = lax.rem(me, 2) == 1
    even = lax.rem(me, 2) == 0
    back = WINDOW
    halves = rows // QROWS
    blocks = rows // CHUNK
    steps = heads // HEADS_STEP
    units = 2 * heads

    both = ((0, ak_hbm, keys), (1, av_hbm, vals))
    far_rows = pl.ds(0, rows)
    near_rows = pl.ds(rows, rows)
    own_rows = pl.ds(back, rows)

    def lanes(h):
        return pl.ds(pl.multiple_of(h * DH, DH), DH)

    def own_copy(h, kind, source, buffer):
        return pltpu.make_async_copy(
            source.at[:, lanes(h)], buffer.at[h, own_rows], own_sem.at[kind, h]
        )

    def far_copy(h, kind, source, buffer):
        return pltpu.make_async_remote_copy(
            src_ref=source.at[:, lanes(h)],
            dst_ref=buffer.at[h, far_rows],
            send_sem=far_send.at[kind, h],
            recv_sem=far_recv.at[kind, h],
            device_id={"ctx": lax.rem(me + 2, contexts)},
            device_id_type=pl.DeviceIdType.MESH,
        )

    def near_copy(h, kind, source, buffer):
        return pltpu.make_async_remote_copy(
            src_ref=source.at[:, lanes(h)],
            dst_ref=buffer.at[h, near_rows],
            send_sem=near_send.at[kind, h],
            recv_sem=near_recv.at[kind, h],
            device_id={"ctx": lax.rem(me + 1, contexts)},
            device_id_type=pl.DeviceIdType.MESH,
        )

    def forward_copy(h, kind, source, buffer):
        return pltpu.make_async_remote_copy(
            src_ref=buffer.at[h, far_rows],
            dst_ref=buffer.at[h, near_rows],
            send_sem=near_send.at[kind, h],
            recv_sem=near_recv.at[kind, h],
            device_id={"ctx": lax.rem(me + contexts - 1, contexts)},
            device_id_type=pl.DeviceIdType.MESH,
        )

    def pair(p):
        return pl.ds(p * HEADS_STEP, HEADS_STEP)

    def relay_copy(p):
        return pltpu.make_async_remote_copy(
            src_ref=leaving.at[pair(p)],
            dst_ref=entering.at[pair(p)],
            send_sem=relay_send.at[p],
            recv_sem=relay_recv.at[p],
            device_id={"ctx": lax.rem(me + 1, contexts)},
            device_id_type=pl.DeviceIdType.MESH,
        )

    def pair_lanes(p):
        return pl.ds(pl.multiple_of(p * HEADS_STEP * DH, HEADS_STEP * DH), HEADS_STEP * DH)

    inputs = ((0, dq_hbm, dq_ref), (1, dk_hbm, dk_ref), (2, dv_hbm, dv_ref))

    def delta_load(p, kind, source, buffer):
        return pltpu.make_async_copy(
            source.at[:, pair_lanes(p)], buffer.at[:, pair_lanes(p)], delta_sem.at[kind, p]
        )

    gate_load = pltpu.make_async_copy(gates_hbm, gates_ref, gates_sem.at[0])
    beta_load = pltpu.make_async_copy(betas_hbm, betas_ref, gates_sem.at[1])
    query_load = pltpu.make_async_copy(aq_hbm, aq_ref, query_sem.at[0])

    def of_unit(u, action):
        h = u // 2
        for args in both:
            @pl.when(lax.rem(u, 2) == args[0])
            def _():
                action(h, *args)

    def send_far(u):
        @pl.when((u < units) & (me + 2 < contexts))
        def _():
            of_unit(u, lambda *args: far_copy(*args).start())

    def send_near(u):
        @pl.when((u < units) & even)
        def _():
            of_unit(u, lambda *args: near_copy(*args).start())

    def send_on(u):
        def action(*args):
            far_copy(*args).wait_recv()
            forward_copy(*args).start()

        @pl.when((u < units) & odd & (me >= 3))
        def _():
            of_unit(u, action)

    def issued(k, ahead):
        early = 3 * steps
        count = (jnp.minimum(k, early) * RATE) // 6 + jnp.maximum(k - early, 0) + ahead
        return jnp.minimum(count, units)

    def advance(k, send, ahead):
        done = jnp.where(k == 0, 0, issued(jnp.maximum(k - 1, 0), ahead))
        lax.fori_loop(done, issued(k, ahead), lambda u, c: (send(u), c)[1], 0)

    def issue(k):
        advance(k, send_far, FAR_AHEAD)
        advance(k, send_near, NEAR_AHEAD)

        @pl.when(k == 1)
        def _():
            advance(0, send_on, PASS_AHEAD)

        advance(k, send_on, PASS_AHEAD)

    gate_load.start()
    beta_load.start()
    for args in inputs:
        delta_load(0, *args).start()

    barrier = pltpu.get_barrier_semaphore()
    for by in (-2, -1, 1, 2):
        @pl.when((me + by >= 0) & (me + by < contexts))
        def _():
            pl.semaphore_signal(
                barrier, inc=1, device_id={"ctx": me + by}, device_id_type=pl.DeviceIdType.MESH
            )
    for by in range(1, groups):
        pl.semaphore_signal(
            barrier, inc=1, device_id={"head": lax.rem(group + by, groups)},
            device_id_type=pl.DeviceIdType.MESH,
        )

    def start_delta(p, carry):
        for args in inputs:
            delta_load(p, *args).start()
        return carry

    lax.fori_loop(1, steps, start_delta, 0)

    near_peers = jnp.minimum(me, 2) + jnp.minimum(contexts - 1 - me, 2)
    pl.semaphore_wait(barrier, near_peers + (groups - 1))

    advance(0, send_far, FAR_AHEAD)
    advance(0, send_near, NEAR_AHEAD)
    query_load.start()
    gain_loads = (
        pltpu.make_async_copy(again_hbm, again_ref, gain_sem.at[0]),
        pltpu.make_async_copy(dgain_hbm, dgain_ref, gain_sem.at[1]),
    )
    for load in gain_loads:
        load.start()

    def start_own(h, carry):
        for args in both:
            own_copy(h, *args).start()
        return carry

    lax.fori_loop(0, heads, start_own, 0)

    @pl.when(me < 2)
    def _():
        def clear(h, carry):
            keys[h, far_rows] = jnp.zeros((rows, DH), bf16)
            vals[h, far_rows] = jnp.zeros((rows, DH), bf16)
            return carry
        lax.fori_loop(0, heads, clear, 0)

    @pl.when(me < 1)
    def _():
        def clear(h, carry):
            keys[h, near_rows] = jnp.zeros((rows, DH), bf16)
            vals[h, near_rows] = jnp.zeros((rows, DH), bf16)
            entering[h] = jnp.zeros((DH, DH), bf16)
            return carry
        lax.fori_loop(0, heads, clear, 0)

    gate_load.wait()
    beta_load.wait()
    for h in range(heads):
        gate_ref[h] = gates_ref[h : h + 1]
        beta_ref[h] = betas_ref[h : h + 1]
    attn_sq[...] = jnp.zeros_like(attn_sq)
    delta_sq[...] = jnp.zeros_like(delta_sq)

    scale = math.log2(math.e) / math.sqrt(DH)
    ri = lax.broadcasted_iota(jnp.int32, (QROWS, QROWS), 0)
    ci = lax.broadcasted_iota(jnp.int32, (QROWS, QROWS), 1)
    tiles = WINDOW // QROWS + 1
    first_tile = jnp.maximum(WINDOW - me * rows, 0) // QROWS

    def attend(h, b):
        q_rows = pl.ds(pl.multiple_of(b * QROWS, QROWS), QROWS)
        q = aq_ref[q_rows, lanes(h)]
        scores = []
        for n in range(tiles):
            at = pl.ds(pl.multiple_of((b + n) * QROWS, QROWS), QROWS)
            s = dot(q, keys[h, at], ((1,), (1,))) * scale
            if n < tiles - 1:
                s = s + jnp.where(b + n >= first_tile, 0.0, -1e30).astype(f32)
            if n == 0:
                s = jnp.where(ci > ri, s, -1e30)
            if n == tiles - 1:
                s = jnp.where(ci <= ri, s, -1e30)
            scores.append(s)
        top = jnp.max(functools.reduce(jnp.maximum, scores), axis=1, keepdims=True)
        raised = [jnp.exp2(s - top) for s in scores]
        total = jnp.sum(functools.reduce(jnp.add, raised), axis=1, keepdims=True)
        inverse = 1.0 / total
        out = None
        for n in range(tiles):
            at = pl.ds(pl.multiple_of((b + n) * QROWS, QROWS), QROWS)
            part = dot((raised[n] * inverse).astype(bf16), vals[h, at])
            out = part if out is None else out + part
        attn_out[h, q_rows] = out
        attn_sq[q_rows, :] += out * out

    def relay(p):
        @pl.when(me >= 1)
        def _():
            relay_copy(p).wait_recv()

        @pl.when(me + 1 < contexts)
        def _():
            for e in range(HEADS_STEP):
                h = p * HEADS_STEP + e
                high, low = split(linear[h])
                state = entering[h]
                leaving[h] = (dot(high, state) + dot(low, state) + offset[h]).astype(bf16)
            relay_copy(p).start()

        for e in range(HEADS_STEP):
            h = p * HEADS_STEP + e
            full = delta_out[h] + dot(qeff[h], entering[h])
            delta_out[h] = full
            delta_sq[...] += full * full

    def service(t):
        q = t - HOP * me

        @pl.when((q >= 0) & (lax.rem(q + 2 * contexts * HOP, 2) == 0) & (q < 2 * steps))
        def _():
            relay(q // 2)

    def step(s, carry):
        early = s < steps
        mark = jnp.where(early, 3 * s, 3 * steps + 2 * (s - steps))

        @pl.when(jnp.logical_not(early))
        def _():
            issue(mark + 1)

        @pl.when(early)
        def _():
            for args in inputs:
                delta_load(s, *args).wait()

            issue(mark + 1)
            delta_heads(
                s * HEADS_STEP, lambda: issue(mark + 2), dq_ref, dk_ref, dv_ref, gate_ref, beta_ref,
                delta_out, qeff, linear, offset,
            )

        service(2 * s)
        h = s - ATTEND_LAG

        @pl.when((h >= 0) & (h < heads))
        def _():
            @pl.when(h == 0)
            def _():
                query_load.wait()

            for args in both:
                own_copy(h, *args).wait()

                @pl.when((me >= 2) & jnp.logical_not(odd & (me >= 3)))
                def _():
                    far_copy(h, *args).wait_recv()

                @pl.when(me >= 1)
                def _():
                    near_copy(h, *args).wait_recv()

            attend(h, 0)

        service(2 * s + 1)
        issue(mark + jnp.where(early, 3, 2))

        @pl.when((h >= 0) & (h < heads))
        def _():
            lax.fori_loop(1, halves, lambda b, c: (attend(h, b), c)[1], 0)

        return carry

    turns = max(heads + ATTEND_LAG, steps + (HOP * (contexts - 1)) // 2, steps + heads)
    lax.fori_loop(0, turns, step, 0)
    for load in gain_loads:
        load.wait()

    dr = lax.broadcasted_iota(jnp.int32, (CHUNK, CHUNK), 0)
    dc = lax.broadcasted_iota(jnp.int32, (CHUNK, CHUNK), 1)
    eye = dr == dc
    lines = []
    for part in (attn_sq, delta_sq):
        for b in range(blocks):
            col = jnp.sum(part[b * CHUNK : (b + 1) * CHUNK, :], axis=1, keepdims=True)
            lines.append(jnp.sum(jnp.where(eye, col, 0.0), axis=0, keepdims=True))
    mine = jnp.concatenate(lines, axis=0)
    sums_send[...] = mine

    def sums_copy(by):
        return pltpu.make_async_remote_copy(
            src_ref=sums_send,
            dst_ref=sums_recv.at[by],
            send_sem=sums_ss.at[by],
            recv_sem=sums_rs.at[by],
            device_id={"head": lax.rem(group + by, groups)},
            device_id_type=pl.DeviceIdType.MESH,
        )

    for by in range(1, groups):
        sums_copy(by).start()
    whole = mine
    for by in range(1, groups):
        sums_copy(by).wait_recv()
        whole = whole + sums_recv[by]
    scales = lax.rsqrt(whole / (width * groups) + epsilon) * 0.5

    for b in range(blocks):
        rs = slice(b * CHUNK, (b + 1) * CHUNK)
        sa = jnp.sum(jnp.where(eye, scales[b : b + 1], 0.0), axis=1, keepdims=True)
        sd = jnp.sum(
            jnp.where(eye, scales[blocks + b : blocks + b + 1], 0.0), axis=1, keepdims=True
        )
        for h in range(heads):
            cs = slice(h * DH, (h + 1) * DH)
            mixed_ref[rs, cs] = (
                again_ref[cs][None, :] * attn_out[h, rs] * sa + dgain_ref[cs][None, :] * delta_out[h, rs] * sd
            ).astype(bf16)

    for by in range(1, groups):
        sums_copy(by).wait_send()

    def drain(h, carry):
        for args in both:
            @pl.when(me + 2 < contexts)
            def _():
                far_copy(h, *args).wait_send()

            @pl.when(even)
            def _():
                near_copy(h, *args).wait_send()

            @pl.when(odd & (me >= 3))
            def _():
                forward_copy(h, *args).wait_send()

        return carry

    lax.fori_loop(0, heads, drain, 0)

    @pl.when(me + 1 < contexts)
    def _():
        lax.fori_loop(0, steps, lambda p, c: (relay_copy(p).wait_send(), c)[1], 0)


def on_device(
    attn_query,
    attn_key,
    attn_value,
    delta_query,
    delta_key,
    delta_value,
    delta_gate,
    delta_beta,
    attn_gain,
    delta_gain,
):
    rows, width = attn_query.shape
    heads = width // DH
    groups = lax.axis_size("head")
    lines = 2 * rows // CHUNK
    hbm = pl.BlockSpec(memory_space=pltpu.HBM)
    dma = pltpu.SemaphoreType.DMA
    return pl.pallas_call(
        functools.partial(layer_kernel, contexts=lax.axis_size("ctx"), groups=groups),
        in_specs=[hbm] * 10,
        out_specs=pl.BlockSpec(memory_space=pltpu.VMEM),
        out_shape=pltpu.VMEM((rows, width), bf16),
        scratch_shapes=[
            pltpu.VMEM((rows, width), bf16),
            pltpu.VMEM((rows, width), bf16),
            pltpu.VMEM((rows, width), bf16),
            pltpu.VMEM((rows, width), bf16),
            pltpu.VMEM((heads, rows), f32),
            pltpu.VMEM((heads, rows), f32),
            pltpu.VMEM((heads, WINDOW + rows, DH), bf16),
            pltpu.VMEM((heads, WINDOW + rows, DH), bf16),
            pltpu.VMEM((heads, rows, DH), f32),
            pltpu.VMEM((heads, rows, DH), f32),
            pltpu.VMEM((heads, rows, DH), bf16),
            pltpu.VMEM((heads, DH, DH), f32),
            pltpu.VMEM((heads, DH, DH), f32),
            pltpu.VMEM((heads, DH, DH), bf16),
            pltpu.VMEM((heads, DH, DH), bf16),
            pltpu.VMEM((rows, DH), f32),
            pltpu.VMEM((rows, DH), f32),
            pltpu.VMEM((lines, CHUNK), f32),
            pltpu.VMEM((groups, lines, CHUNK), f32),
            pltpu.VMEM((heads, 1, rows), f32),
            pltpu.VMEM((heads, 1, rows), f32),
            pltpu.VMEM((width,), f32),
            pltpu.VMEM((width,), f32),
            dma((2,)),
            dma((2, heads)),
            dma((2, heads)),
            dma((2, heads)),
            dma((2, heads)),
            dma((2, heads)),
            dma((heads // HEADS_STEP,)),
            dma((heads // HEADS_STEP,)),
            dma((groups,)),
            dma((groups,)),
            dma((1,)),
            dma((2,)),
            dma((3, heads // HEADS_STEP)),
        ],
        compiler_params=pltpu.CompilerParams(
            collective_id=0, has_side_effects=True, vmem_limit_bytes=67043328 - 2 * rows * width - 16384
        ),
        name="layer",
    )(
        attn_query,
        attn_key,
        attn_value,
        delta_query,
        delta_key,
        delta_value,
        delta_gate.T,
        delta_beta.T,
        attn_gain,
        delta_gain,
    )


def solution(mesh):
    both = P("ctx", "head")
    return jax.shard_map(
        on_device,
        mesh=mesh,
        in_specs=(both,) * 8 + (P("head"),) * 2,
        out_specs=both,
        check_vma=False,
    )
```

```python
import functools
import math

import jax
import jax.numpy as jnp
from jax import lax
from jax.experimental import pallas as pl
from jax.experimental.pallas import tpu as pltpu
from jax.sharding import PartitionSpec as P

DH = 128
WINDOW = 1024
CHUNK = 128
QROWS = 256
FAR_AHEAD = 3
NEAR_AHEAD = 1
PASS_AHEAD = 1
ATTEND_LAG = 1
LATE_STRIDE = 3
RATE = 5
STAGE_AT = 6
HEADS_STEP = 2

epsilon = 1e-06
f32 = jnp.float32
bf16 = jnp.bfloat16


def dot(left, right, dims=((1,), (0,))):
    return lax.dot_general(left, right, (dims, ((), ())), preferred_element_type=f32)


def dot1(left, right, dims=((1,), (0,))):
    return dot(left.astype(bf16), right.astype(bf16), dims)


def split(value):
    high = value.astype(bf16)
    return high, (value - high.astype(f32)).astype(bf16)


def dot3(left, right, dims=((1,), (0,))):
    lh, ll = split(left)
    rh, rl = split(right)
    return dot(lh, rh, dims) + (dot(lh, rl, dims) + dot(ll, rh, dims))


def unit_scale(raw):
    wide = raw.astype(f32)
    mean = jnp.mean(wide * wide, axis=-1, keepdims=True)
    return lax.rsqrt(mean + epsilon) / math.sqrt(DH)


def delta_heads(first, between, q_ref, k_ref, v_ref, gate_ref, beta_ref, out_ref, qeff_ref, lin_ref, off_ref):
    rows = q_ref.shape[0]
    chunks = rows // CHUNK
    ri = lax.broadcasted_iota(jnp.int32, (CHUNK, CHUNK), 0)
    ci = lax.broadcasted_iota(jnp.int32, (CHUNK, CHUNK), 1)
    eye = ri == ci
    lower = ri >= ci
    strict = ri > ci
    identity = jnp.where(eye, 1.0, 0.0).astype(f32)

    def column(row):
        return jnp.sum(jnp.where(eye, row, 0.0), axis=1, keepdims=True)

    def as_row(col):
        return jnp.sum(jnp.where(eye, col, 0.0), axis=0, keepdims=True)

    units = [(h, c) for c in range(chunks) for h in range(HEADS_STEP)]
    terms = {}
    for h, c in units:
        rs = slice(c * CHUNK, (c + 1) * CHUNK)
        cs = pl.ds(pl.multiple_of((first + h) * DH, DH), DH)
        q, k = q_ref[rs, cs], k_ref[rs, cs]
        log_row = jnp.log(gate_ref[first + h, :, rs])
        log_col = column(log_row)
        beta_col = column(beta_ref[first + h, :, rs])
        sum_row = jnp.sum(jnp.where(ri <= ci, log_col, 0.0), axis=0, keepdims=True)
        sum_col = jnp.sum(jnp.where(lower, log_row, 0.0), axis=1, keepdims=True)
        total = jnp.sum(log_row, axis=1, keepdims=True)
        sk, sq = unit_scale(k), unit_scale(q)
        sk_row = as_row(sk)
        ratios = jnp.exp(jnp.where(lower, sum_col - sum_row, -1e30)) * sk_row
        both = dot(jnp.concatenate([k, q], axis=0), k, ((1,), (1,)))
        low = jnp.where(strict, (beta_col * sk) * ratios * both[:CHUNK], 0.0)
        mix = (sq * ratios) * both[CHUNK:]
        growth = jnp.exp(sum_col)
        terms[h, c] = dict(
            low=low,
            mix=mix.astype(bf16),
            inv=identity - jnp.where((ri // 2) == (ci // 2), low, 0.0),
            beta=beta_col,
            gk=growth * sk,
            gq=growth * sq,
            tail=jnp.exp(total - sum_col) * sk,
            last=jnp.exp(total),
        )
    size = 2
    while size < CHUNK:
        pick = ((ri // (2 * size)) == (ci // (2 * size))) & ((ri // size) != (ci // size))
        for u in units:
            t = terms[u]
            t["tmp"] = dot1(jnp.where(pick, t["low"], 0.0), t["inv"])
        for u in units:
            t = terms[u]
            t["inv"] = t["inv"] - dot1(t["inv"], t["tmp"])
        size *= 2
    between()
    states = [None] * HEADS_STEP
    for c in range(chunks):
        rs = slice(c * CHUNK, (c + 1) * CHUNK)
        for h in range(HEADS_STEP):
            cs = pl.ds(pl.multiple_of((first + h) * DH, DH), DH)
            t = terms[h, c]
            q, k, v = q_ref[rs, cs], k_ref[rs, cs], v_ref[rs, cs].astype(f32)
            zero = jnp.zeros((CHUNK, DH), f32)
            if c == 0:
                state = jnp.concatenate([jnp.zeros((DH, DH), f32), identity], axis=1)
                ks = jnp.concatenate([zero, k.astype(f32)], axis=1)
                qs = jnp.concatenate([zero, q.astype(f32)], axis=1)
            else:
                state = states[h]
                sb = state.astype(bf16)
                kqs = dot(jnp.concatenate([k, q], axis=0), sb)
                ks, qs = kqs[:CHUNK], kqs[CHUNK:]
            resid = jnp.concatenate([v, zero], axis=1) - t["gk"] * ks
            errors = dot1(t["inv"], t["beta"] * resid)
            out = t["gq"] * qs + dot(t["mix"], errors.astype(bf16))
            out_ref[first + h, rs] = out[:, :DH]
            qeff_ref[first + h, rs] = out[:, DH:].astype(bf16)
            states[h] = t["last"] * state + dot(
                k, (t["tail"] * errors).astype(bf16), ((0,), (0,))
            )
    for h in range(HEADS_STEP):
        off_ref[first + h] = states[h][:, :DH]
        lin_ref[first + h] = states[h][:, DH:]


def layer_kernel(
    aq_hbm, ak_hbm, av_hbm, dq_hbm, dk_hbm, dv_hbm, gates_hbm, betas_hbm, again_hbm, dgain_hbm,
    mixed_ref,
    aq_ref, dq_ref, dk_ref, dv_ref, gates_ref, betas_ref,
    keys, vals, attn_out, delta_out, qeff, linear, offset, entering, leaving, attn_sq, delta_sq,
    sums_send, sums_recv, gate_ref, beta_ref, again_ref, dgain_ref,
    gain_sem, own_sem, far_send, far_recv, near_send, near_recv, relay_send, relay_recv, sums_ss, sums_rs,
    query_sem, gates_sem, delta_sem, stage, stage_send, stage_recv, hop_send,
    *, contexts, groups,
):
    rows, width = aq_hbm.shape
    heads = width // DH
    me = lax.axis_index("ctx")
    group = lax.axis_index("head")
    odd = lax.rem(me, 2) == 1
    even = lax.rem(me, 2) == 0
    back = WINDOW
    halves = rows // QROWS
    blocks = rows // CHUNK
    steps = heads // HEADS_STEP
    units = 2 * heads

    both = ((0, ak_hbm, keys), (1, av_hbm, vals))
    far_rows = pl.ds(0, rows)
    near_rows = pl.ds(rows, rows)
    own_rows = pl.ds(back, rows)

    def lanes(h):
        return pl.ds(pl.multiple_of(h * DH, DH), DH)

    def own_copy(h, kind, source, buffer):
        return pltpu.make_async_copy(
            source.at[:, lanes(h)], buffer.at[h, own_rows], own_sem.at[kind, h]
        )

    def far_copy(h, kind, source, buffer):
        return pltpu.make_async_remote_copy(
            src_ref=source.at[:, lanes(h)],
            dst_ref=buffer.at[h, far_rows],
            send_sem=far_send.at[kind, h],
            recv_sem=far_recv.at[kind, h],
            device_id={"ctx": lax.rem(me + 2, contexts)},
            device_id_type=pl.DeviceIdType.MESH,
        )

    def near_copy(h, kind, source, buffer):
        return pltpu.make_async_remote_copy(
            src_ref=source.at[:, lanes(h)],
            dst_ref=buffer.at[h, near_rows],
            send_sem=near_send.at[kind, h],
            recv_sem=near_recv.at[kind, h],
            device_id={"ctx": lax.rem(me + 1, contexts)},
            device_id_type=pl.DeviceIdType.MESH,
        )

    def forward_copy(h, kind, source, buffer):
        return pltpu.make_async_remote_copy(
            src_ref=buffer.at[h, far_rows],
            dst_ref=buffer.at[h, near_rows],
            send_sem=near_send.at[kind, h],
            recv_sem=near_recv.at[kind, h],
            device_id={"ctx": lax.rem(me + contexts - 1, contexts)},
            device_id_type=pl.DeviceIdType.MESH,
        )

    def stage_copy(kind, source, buffer):
        return pltpu.make_async_remote_copy(
            src_ref=source.at[:, lanes(heads - 1)],
            dst_ref=stage.at[kind],
            send_sem=stage_send.at[kind],
            recv_sem=stage_recv.at[kind],
            device_id={"ctx": lax.rem(me + contexts - 1, contexts)},
            device_id_type=pl.DeviceIdType.MESH,
        )

    def hop_copy(kind, source, buffer):
        return pltpu.make_async_remote_copy(
            src_ref=stage.at[kind],
            dst_ref=buffer.at[heads - 1, near_rows],
            send_sem=hop_send.at[kind],
            recv_sem=near_recv.at[kind, heads - 1],
            device_id={"ctx": lax.rem(me + 2, contexts)},
            device_id_type=pl.DeviceIdType.MESH,
        )

    stages = odd & (me + 1 < contexts)
    hops = even & (me + 2 < contexts)

    def pair(p):
        return pl.ds(p * HEADS_STEP, HEADS_STEP)

    def relay_copy(p):
        return pltpu.make_async_remote_copy(
            src_ref=leaving.at[pair(p)],
            dst_ref=entering.at[pair(p)],
            send_sem=relay_send.at[p],
            recv_sem=relay_recv.at[p],
            device_id={"ctx": lax.rem(me + 1, contexts)},
            device_id_type=pl.DeviceIdType.MESH,
        )

    def pair_lanes(p):
        return pl.ds(pl.multiple_of(p * HEADS_STEP * DH, HEADS_STEP * DH), HEADS_STEP * DH)

    inputs = ((0, dq_hbm, dq_ref), (1, dk_hbm, dk_ref), (2, dv_hbm, dv_ref))

    def delta_load(p, kind, source, buffer):
        return pltpu.make_async_copy(
            source.at[:, pair_lanes(p)], buffer.at[:, pair_lanes(p)], delta_sem.at[kind, p]
        )

    gate_load = pltpu.make_async_copy(gates_hbm, gates_ref, gates_sem.at[0])
    beta_load = pltpu.make_async_copy(betas_hbm, betas_ref, gates_sem.at[1])
    query_load = pltpu.make_async_copy(aq_hbm, aq_ref, query_sem.at[0])

    def of_unit(u, action):
        h = u // 2
        for args in both:
            @pl.when(lax.rem(u, 2) == args[0])
            def _():
                action(h, *args)

    def send_far(u):
        @pl.when((u < units) & (me + 2 < contexts))
        def _():
            of_unit(u, lambda *args: far_copy(*args).start())

    def send_near(u):
        @pl.when((u < units) & even)
        def _():
            of_unit(u, lambda *args: near_copy(*args).start())

    def send_on(u):
        def action(*args):
            far_copy(*args).wait_recv()
            forward_copy(*args).start()

        @pl.when((u < units - 2) & odd & (me >= 3))
        def _():
            of_unit(u, action)

    def issued(k, ahead):
        early = 3 * steps
        count = (jnp.minimum(k, early) * RATE) // 6 + jnp.maximum(k - early, 0) + ahead
        return jnp.minimum(count, units)

    def advance(k, send, ahead):
        done = jnp.where(k == 0, 0, issued(jnp.maximum(k - 1, 0), ahead))
        lax.fori_loop(done, issued(k, ahead), lambda u, c: (send(u), c)[1], 0)

    def issue_free(k):
        @pl.when(even)
        def _():
            advance(k, send_far, FAR_AHEAD)

        @pl.when(k == 1)
        def _():
            advance(0, send_on, PASS_AHEAD)

        advance(k, send_on, PASS_AHEAD)

        @pl.when((k == STAGE_AT) & hops)
        def _():
            for args in both:
                stage_copy(*args).wait_recv()
                hop_copy(*args).start()

    def issue_tight(k):
        @pl.when(odd)
        def _():
            advance(k, send_far, FAR_AHEAD)

        advance(k, send_near, NEAR_AHEAD)

    def issue(k):
        issue_tight(k)
        issue_free(k)

    gate_load.start()
    beta_load.start()
    for args in inputs:
        delta_load(0, *args).start()

    barrier = pltpu.get_barrier_semaphore()
    for by in (-2, -1, 1, 2):
        @pl.when((me + by >= 0) & (me + by < contexts))
        def _():
            pl.semaphore_signal(
                barrier, inc=1, device_id={"ctx": me + by}, device_id_type=pl.DeviceIdType.MESH
            )
    for by in range(1, groups):
        pl.semaphore_signal(
            barrier, inc=1, device_id={"head": lax.rem(group + by, groups)},
            device_id_type=pl.DeviceIdType.MESH,
        )

    def start_delta(p, carry):
        for args in inputs:
            delta_load(p, *args).start()
        return carry

    lax.fori_loop(1, steps, start_delta, 0)

    near_peers = jnp.minimum(me, 2) + jnp.minimum(contexts - 1 - me, 2)
    pl.semaphore_wait(barrier, near_peers + (groups - 1))

    @pl.when(stages)
    def _():
        for args in both:
            stage_copy(*args).start()

    advance(0, send_far, FAR_AHEAD)
    advance(0, send_near, NEAR_AHEAD)
    query_load.start()
    gain_loads = (
        pltpu.make_async_copy(again_hbm, again_ref, gain_sem.at[0]),
        pltpu.make_async_copy(dgain_hbm, dgain_ref, gain_sem.at[1]),
    )
    for load in gain_loads:
        load.start()

    def start_own(h, carry):
        for args in both:
            own_copy(h, *args).start()
        return carry

    lax.fori_loop(0, heads, start_own, 0)

    @pl.when(me < 2)
    def _():
        def clear(h, carry):
            keys[h, far_rows] = jnp.zeros((rows, DH), bf16)
            vals[h, far_rows] = jnp.zeros((rows, DH), bf16)
            return carry
        lax.fori_loop(0, heads, clear, 0)

    @pl.when(me < 1)
    def _():
        def clear(h, carry):
            keys[h, near_rows] = jnp.zeros((rows, DH), bf16)
            vals[h, near_rows] = jnp.zeros((rows, DH), bf16)
            entering[h] = jnp.zeros((DH, DH), bf16)
            return carry
        lax.fori_loop(0, heads, clear, 0)

    gate_load.wait()
    beta_load.wait()
    for h in range(heads):
        gate_ref[h] = gates_ref[h : h + 1]
        beta_ref[h] = betas_ref[h : h + 1]
    attn_sq[...] = jnp.zeros_like(attn_sq)
    delta_sq[...] = jnp.zeros_like(delta_sq)

    scale = math.log2(math.e) / math.sqrt(DH)
    ri = lax.broadcasted_iota(jnp.int32, (QROWS, QROWS), 0)
    ci = lax.broadcasted_iota(jnp.int32, (QROWS, QROWS), 1)
    tiles = WINDOW // QROWS + 1
    first_tile = jnp.maximum(WINDOW - me * rows, 0) // QROWS

    def attend(h, b):
        q_rows = pl.ds(pl.multiple_of(b * QROWS, QROWS), QROWS)
        q = aq_ref[q_rows, lanes(h)]
        scores = []
        for n in range(tiles):
            at = pl.ds(pl.multiple_of((b + n) * QROWS, QROWS), QROWS)
            s = dot(q, keys[h, at], ((1,), (1,))) * scale
            if n < tiles - 1:
                s = s + jnp.where(b + n >= first_tile, 0.0, -1e30).astype(f32)
            if n == 0:
                s = jnp.where(ci > ri, s, -1e30)
            if n == tiles - 1:
                s = jnp.where(ci <= ri, s, -1e30)
            scores.append(s)
        top = jnp.max(functools.reduce(jnp.maximum, scores), axis=1, keepdims=True)
        raised = [jnp.exp2(s - top) for s in scores]
        total = jnp.sum(functools.reduce(jnp.add, raised), axis=1, keepdims=True)
        inverse = 1.0 / total
        out = None
        for n in range(tiles):
            at = pl.ds(pl.multiple_of((b + n) * QROWS, QROWS), QROWS)
            part = dot((raised[n] * inverse).astype(bf16), vals[h, at])
            out = part if out is None else out + part
        attn_out[h, q_rows] = out
        attn_sq[q_rows, :] += out * out

    def relay(p):
        @pl.when(me >= 1)
        def _():
            relay_copy(p).wait_recv()

        @pl.when(me + 1 < contexts)
        def _():
            for e in range(HEADS_STEP):
                h = p * HEADS_STEP + e
                high, low = split(linear[h])
                state = entering[h]
                leaving[h] = (dot(high, state) + dot(low, state) + offset[h]).astype(bf16)
            relay_copy(p).start()

        for e in range(HEADS_STEP):
            h = p * HEADS_STEP + e
            full = delta_out[h] + dot(qeff[h], entering[h])
            delta_out[h] = full
            delta_sq[...] += full * full

    def service(t):
        over = t - 2 * steps
        late = over >= 0
        turn = jnp.where(late, 2 * steps + over // LATE_STRIDE, t)
        q = turn - me

        @pl.when(
            (q >= 0) & (lax.rem(q + 2 * contexts, 2) == 0) & (q < 2 * steps)
            & (jnp.logical_not(late) | (lax.rem(over + 2 * steps * LATE_STRIDE, LATE_STRIDE) == 0))
        )
        def _():
            relay(q // 2)

    def step(s, carry):
        early = s < steps
        mark = jnp.where(early, 3 * s, 3 * steps + 2 * (s - steps))

        @pl.when(jnp.logical_not(early))
        def _():
            issue(mark + 1)

        @pl.when(early)
        def _():
            for args in inputs:
                delta_load(s, *args).wait()

            issue(mark + 1)
            delta_heads(
                s * HEADS_STEP, lambda: issue(mark + 2), dq_ref, dk_ref, dv_ref, gate_ref, beta_ref,
                delta_out, qeff, linear, offset,
            )

        service(2 * s)
        h = s - ATTEND_LAG

        @pl.when((h >= 0) & (h < heads))
        def _():
            @pl.when(h == 0)
            def _():
                query_load.wait()

            for args in both:
                own_copy(h, *args).wait()

                @pl.when((me >= 2) & jnp.logical_not(odd & (me >= 3) & (h < heads - 1)))
                def _():
                    far_copy(h, *args).wait_recv()

                @pl.when(me >= 1)
                def _():
                    near_copy(h, *args).wait_recv()

            attend(h, 0)

        third = mark + jnp.where(early, 3, 2)
        issue_free(third)
        service(2 * s + 1)
        issue_tight(third)

        @pl.when((h >= 0) & (h < heads))
        def _():
            lax.fori_loop(1, halves, lambda b, c: (attend(h, b), c)[1], 0)

        return carry

    last_turn = max(2 * (steps - 1) + contexts - 1 - 2 * steps, 0)
    turns = max(heads + ATTEND_LAG, steps + heads, steps + (last_turn * LATE_STRIDE) // 2 + 1)
    lax.fori_loop(0, turns, step, 0)
    for load in gain_loads:
        load.wait()

    dr = lax.broadcasted_iota(jnp.int32, (CHUNK, CHUNK), 0)
    dc = lax.broadcasted_iota(jnp.int32, (CHUNK, CHUNK), 1)
    eye = dr == dc
    lines = []
    for part in (attn_sq, delta_sq):
        for b in range(blocks):
            col = jnp.sum(part[b * CHUNK : (b + 1) * CHUNK, :], axis=1, keepdims=True)
            lines.append(jnp.sum(jnp.where(eye, col, 0.0), axis=0, keepdims=True))
    mine = jnp.concatenate(lines, axis=0)
    sums_send[...] = mine

    def sums_copy(by):
        return pltpu.make_async_remote_copy(
            src_ref=sums_send,
            dst_ref=sums_recv.at[by],
            send_sem=sums_ss.at[by],
            recv_sem=sums_rs.at[by],
            device_id={"head": lax.rem(group + by, groups)},
            device_id_type=pl.DeviceIdType.MESH,
        )

    for by in range(1, groups):
        sums_copy(by).start()
    whole = mine
    for by in range(1, groups):
        sums_copy(by).wait_recv()
        whole = whole + sums_recv[by]
    scales = lax.rsqrt(whole / (width * groups) + epsilon) * 0.5

    for b in range(blocks):
        rs = slice(b * CHUNK, (b + 1) * CHUNK)
        sa = jnp.sum(jnp.where(eye, scales[b : b + 1], 0.0), axis=1, keepdims=True)
        sd = jnp.sum(
            jnp.where(eye, scales[blocks + b : blocks + b + 1], 0.0), axis=1, keepdims=True
        )
        for h in range(heads):
            cs = slice(h * DH, (h + 1) * DH)
            mixed_ref[rs, cs] = (
                again_ref[cs][None, :] * attn_out[h, rs] * sa + dgain_ref[cs][None, :] * delta_out[h, rs] * sd
            ).astype(bf16)

    for by in range(1, groups):
        sums_copy(by).wait_send()

    def drain(h, carry):
        for args in both:
            @pl.when(me + 2 < contexts)
            def _():
                far_copy(h, *args).wait_send()

            @pl.when(even)
            def _():
                near_copy(h, *args).wait_send()

            @pl.when(odd & (me >= 3) & (h < heads - 1))
            def _():
                forward_copy(h, *args).wait_send()

            @pl.when((h == 0) & stages)
            def _():
                stage_copy(*args).wait_send()

            @pl.when((h == 0) & hops)
            def _():
                hop_copy(*args).wait_send()

        return carry

    lax.fori_loop(0, heads, drain, 0)

    @pl.when(me + 1 < contexts)
    def _():
        lax.fori_loop(0, steps, lambda p, c: (relay_copy(p).wait_send(), c)[1], 0)


def on_device(
    attn_query,
    attn_key,
    attn_value,
    delta_query,
    delta_key,
    delta_value,
    delta_gate,
    delta_beta,
    attn_gain,
    delta_gain,
):
    rows, width = attn_query.shape
    heads = width // DH
    groups = lax.axis_size("head")
    lines = 2 * rows // CHUNK
    hbm = pl.BlockSpec(memory_space=pltpu.HBM)
    dma = pltpu.SemaphoreType.DMA
    return pl.pallas_call(
        functools.partial(layer_kernel, contexts=lax.axis_size("ctx"), groups=groups),
        in_specs=[hbm] * 10,
        out_specs=pl.BlockSpec(memory_space=pltpu.VMEM),
        out_shape=pltpu.VMEM((rows, width), bf16),
        scratch_shapes=[
            pltpu.VMEM((rows, width), bf16),
            pltpu.VMEM((rows, width), bf16),
            pltpu.VMEM((rows, width), bf16),
            pltpu.VMEM((rows, width), bf16),
            pltpu.VMEM((heads, rows), f32),
            pltpu.VMEM((heads, rows), f32),
            pltpu.VMEM((heads, WINDOW + rows, DH), bf16),
            pltpu.VMEM((heads, WINDOW + rows, DH), bf16),
            pltpu.VMEM((heads, rows, DH), f32),
            pltpu.VMEM((heads, rows, DH), f32),
            pltpu.VMEM((heads, rows, DH), bf16),
            pltpu.VMEM((heads, DH, DH), f32),
            pltpu.VMEM((heads, DH, DH), f32),
            pltpu.VMEM((heads, DH, DH), bf16),
            pltpu.VMEM((heads, DH, DH), bf16),
            pltpu.VMEM((rows, DH), f32),
            pltpu.VMEM((rows, DH), f32),
            pltpu.VMEM((lines, CHUNK), f32),
            pltpu.VMEM((groups, lines, CHUNK), f32),
            pltpu.VMEM((heads, 1, rows), f32),
            pltpu.VMEM((heads, 1, rows), f32),
            pltpu.VMEM((width,), f32),
            pltpu.VMEM((width,), f32),
            dma((2,)),
            dma((2, heads)),
            dma((2, heads)),
            dma((2, heads)),
            dma((2, heads)),
            dma((2, heads)),
            dma((heads // HEADS_STEP,)),
            dma((heads // HEADS_STEP,)),
            dma((groups,)),
            dma((groups,)),
            dma((1,)),
            dma((2,)),
            dma((3, heads // HEADS_STEP)),
            pltpu.VMEM((2, rows, DH), bf16),
            dma((2,)),
            dma((2,)),
            dma((2,)),
        ],
        compiler_params=pltpu.CompilerParams(
            collective_id=0, has_side_effects=True, vmem_limit_bytes=67043328 - 2 * rows * width - 16384
        ),
        name="layer",
    )(
        attn_query,
        attn_key,
        attn_value,
        delta_query,
        delta_key,
        delta_value,
        delta_gate.T,
        delta_beta.T,
        attn_gain,
        delta_gain,
    )


def solution(mesh):
    both = P("ctx", "head")
    return jax.shard_map(
        on_device,
        mesh=mesh,
        in_specs=(both,) * 8 + (P("head"),) * 2,
        out_specs=both,
        check_vma=False,
    )
```

```python
import functools
import math

import jax
import jax.numpy as jnp
from jax import lax
from jax.experimental import pallas as pl
from jax.experimental.pallas import tpu as pltpu
from jax.sharding import PartitionSpec as P

DH = 128
WINDOW = 1024
CHUNK = 128
QROWS = 256
FAR_AHEAD = 3
NEAR_AHEAD = 1
PASS_AHEAD = 1
ATTEND_LAG = 1
LATE_STRIDE = 3
RATE = 5
STAGE_AT = 6
HEADS_STEP = 2

epsilon = 1e-06
f32 = jnp.float32
bf16 = jnp.bfloat16


def dot(left, right, dims=((1,), (0,))):
    return lax.dot_general(left, right, (dims, ((), ())), preferred_element_type=f32)


def dot1(left, right, dims=((1,), (0,))):
    return dot(left.astype(bf16), right.astype(bf16), dims)


def split(value):
    high = value.astype(bf16)
    return high, (value - high.astype(f32)).astype(bf16)


def dot3(left, right, dims=((1,), (0,))):
    lh, ll = split(left)
    rh, rl = split(right)
    return dot(lh, rh, dims) + (dot(lh, rl, dims) + dot(ll, rh, dims))


def unit_scale(raw):
    wide = raw.astype(f32)
    mean = jnp.mean(wide * wide, axis=-1, keepdims=True)
    return lax.rsqrt(mean + epsilon) / math.sqrt(DH)


def delta_heads(first, between, q_ref, k_ref, v_ref, gate_ref, beta_ref, out_ref, qeff_ref, lin_ref, off_ref):
    rows = q_ref.shape[0]
    chunks = rows // CHUNK
    ri = lax.broadcasted_iota(jnp.int32, (CHUNK, CHUNK), 0)
    ci = lax.broadcasted_iota(jnp.int32, (CHUNK, CHUNK), 1)
    eye = ri == ci
    lower = ri >= ci
    strict = ri > ci
    identity = jnp.where(eye, 1.0, 0.0).astype(f32)

    def column(row):
        return jnp.sum(jnp.where(eye, row, 0.0), axis=1, keepdims=True)

    def as_row(col):
        return jnp.sum(jnp.where(eye, col, 0.0), axis=0, keepdims=True)

    units = [(h, c) for c in range(chunks) for h in range(HEADS_STEP)]
    terms = {}
    for h, c in units:
        rs = slice(c * CHUNK, (c + 1) * CHUNK)
        cs = pl.ds(pl.multiple_of((first + h) * DH, DH), DH)
        q, k = q_ref[rs, cs], k_ref[rs, cs]
        log_row = jnp.log(gate_ref[first + h, :, rs])
        log_col = column(log_row)
        beta_col = column(beta_ref[first + h, :, rs])
        sum_row = jnp.sum(jnp.where(ri <= ci, log_col, 0.0), axis=0, keepdims=True)
        sum_col = jnp.sum(jnp.where(lower, log_row, 0.0), axis=1, keepdims=True)
        total = jnp.sum(log_row, axis=1, keepdims=True)
        sk, sq = unit_scale(k), unit_scale(q)
        sk_row = as_row(sk)
        ratios = jnp.exp(jnp.where(lower, sum_col - sum_row, -1e30)) * sk_row
        both = dot(jnp.concatenate([k, q], axis=0), k, ((1,), (1,)))
        low = jnp.where(strict, (beta_col * sk) * ratios * both[:CHUNK], 0.0)
        mix = (sq * ratios) * both[CHUNK:]
        growth = jnp.exp(sum_col)
        terms[h, c] = dict(
            low=low,
            mix=mix.astype(bf16),
            inv=identity - jnp.where((ri // 2) == (ci // 2), low, 0.0),
            beta=beta_col,
            gk=growth * sk,
            gq=growth * sq,
            tail=jnp.exp(total - sum_col) * sk,
            last=jnp.exp(total),
        )
    size = 2
    while size < CHUNK:
        pick = ((ri // (2 * size)) == (ci // (2 * size))) & ((ri // size) != (ci // size))
        for u in units:
            t = terms[u]
            t["tmp"] = dot1(jnp.where(pick, t["low"], 0.0), t["inv"])
        for u in units:
            t = terms[u]
            t["inv"] = t["inv"] - dot1(t["inv"], t["tmp"])
        size *= 2
    between()
    states = [None] * HEADS_STEP
    for c in range(chunks):
        rs = slice(c * CHUNK, (c + 1) * CHUNK)
        for h in range(HEADS_STEP):
            cs = pl.ds(pl.multiple_of((first + h) * DH, DH), DH)
            t = terms[h, c]
            q, k, v = q_ref[rs, cs], k_ref[rs, cs], v_ref[rs, cs].astype(f32)
            zero = jnp.zeros((CHUNK, DH), f32)
            if c == 0:
                state = jnp.concatenate([jnp.zeros((DH, DH), f32), identity], axis=1)
                ks = jnp.concatenate([zero, k.astype(f32)], axis=1)
                qs = jnp.concatenate([zero, q.astype(f32)], axis=1)
            else:
                state = states[h]
                sb = state.astype(bf16)
                kqs = dot(jnp.concatenate([k, q], axis=0), sb)
                ks, qs = kqs[:CHUNK], kqs[CHUNK:]
            resid = jnp.concatenate([v, zero], axis=1) - t["gk"] * ks
            errors = dot1(t["inv"], t["beta"] * resid)
            out = t["gq"] * qs + dot(t["mix"], errors.astype(bf16))
            out_ref[first + h, rs] = out[:, :DH]
            qeff_ref[first + h, rs] = out[:, DH:].astype(bf16)
            states[h] = t["last"] * state + dot(
                k, (t["tail"] * errors).astype(bf16), ((0,), (0,))
            )
    for h in range(HEADS_STEP):
        off_ref[first + h] = states[h][:, :DH]
        lin_ref[first + h] = states[h][:, DH:]


def layer_kernel(
    aq_hbm, ak_hbm, av_hbm, dq_hbm, dk_hbm, dv_hbm, gates_hbm, betas_hbm, again_hbm, dgain_hbm,
    mixed_ref,
    aq_ref, dq_ref, dk_ref, dv_ref, gates_ref, betas_ref,
    keys, vals, attn_out, delta_out, qeff, linear, offset, entering, leaving, attn_sq, delta_sq,
    sums_send, sums_recv, gate_ref, beta_ref, again_ref, dgain_ref,
    gain_sem, own_sem, far_send, far_recv, near_send, near_recv, relay_send, relay_recv, sums_ss, sums_rs,
    query_sem, gates_sem, delta_sem, stage, stage_send, stage_recv, hop_send,
    *, contexts, groups,
):
    rows, width = aq_hbm.shape
    heads = width // DH
    me = lax.axis_index("ctx")
    group = lax.axis_index("head")
    odd = lax.rem(me, 2) == 1
    even = lax.rem(me, 2) == 0
    back = WINDOW
    halves = rows // QROWS
    blocks = rows // CHUNK
    steps = heads // HEADS_STEP
    units = 2 * heads

    both = ((0, ak_hbm, keys), (1, av_hbm, vals))
    far_rows = pl.ds(0, rows)
    near_rows = pl.ds(rows, rows)
    own_rows = pl.ds(back, rows)

    def lanes(h):
        return pl.ds(pl.multiple_of(h * DH, DH), DH)

    def own_copy(h, kind, source, buffer):
        return pltpu.make_async_copy(
            source.at[:, lanes(h)], buffer.at[h, own_rows], own_sem.at[kind, h]
        )

    def far_copy(h, kind, source, buffer):
        return pltpu.make_async_remote_copy(
            src_ref=source.at[:, lanes(h)],
            dst_ref=buffer.at[h, far_rows],
            send_sem=far_send.at[kind, h],
            recv_sem=far_recv.at[kind, h],
            device_id={"ctx": lax.rem(me + 2, contexts)},
            device_id_type=pl.DeviceIdType.MESH,
        )

    def near_copy(h, kind, source, buffer):
        return pltpu.make_async_remote_copy(
            src_ref=source.at[:, lanes(h)],
            dst_ref=buffer.at[h, near_rows],
            send_sem=near_send.at[kind, h],
            recv_sem=near_recv.at[kind, h],
            device_id={"ctx": lax.rem(me + 1, contexts)},
            device_id_type=pl.DeviceIdType.MESH,
        )

    def forward_copy(h, kind, source, buffer):
        return pltpu.make_async_remote_copy(
            src_ref=buffer.at[h, far_rows],
            dst_ref=buffer.at[h, near_rows],
            send_sem=near_send.at[kind, h],
            recv_sem=near_recv.at[kind, h],
            device_id={"ctx": lax.rem(me + contexts - 1, contexts)},
            device_id_type=pl.DeviceIdType.MESH,
        )

    def stage_copy(kind, source, buffer):
        return pltpu.make_async_remote_copy(
            src_ref=source.at[:, lanes(heads - 1)],
            dst_ref=stage.at[kind],
            send_sem=stage_send.at[kind],
            recv_sem=stage_recv.at[kind],
            device_id={"ctx": lax.rem(me + contexts - 1, contexts)},
            device_id_type=pl.DeviceIdType.MESH,
        )

    def hop_copy(kind, source, buffer):
        return pltpu.make_async_remote_copy(
            src_ref=stage.at[kind],
            dst_ref=buffer.at[heads - 1, near_rows],
            send_sem=hop_send.at[kind],
            recv_sem=near_recv.at[kind, heads - 1],
            device_id={"ctx": lax.rem(me + 2, contexts)},
            device_id_type=pl.DeviceIdType.MESH,
        )

    stages = odd & (me + 1 < contexts)
    hops = even & (me + 2 < contexts)

    def pair(p):
        return pl.ds(p * HEADS_STEP, HEADS_STEP)

    def relay_copy(p):
        return pltpu.make_async_remote_copy(
            src_ref=leaving.at[pair(p)],
            dst_ref=entering.at[pair(p)],
            send_sem=relay_send.at[p],
            recv_sem=relay_recv.at[p],
            device_id={"ctx": lax.rem(me + 1, contexts)},
            device_id_type=pl.DeviceIdType.MESH,
        )

    def pair_lanes(p):
        return pl.ds(pl.multiple_of(p * HEADS_STEP * DH, HEADS_STEP * DH), HEADS_STEP * DH)

    inputs = ((0, dq_hbm, dq_ref), (1, dk_hbm, dk_ref), (2, dv_hbm, dv_ref))

    def delta_load(p, kind, source, buffer):
        return pltpu.make_async_copy(
            source.at[:, pair_lanes(p)], buffer.at[:, pair_lanes(p)], delta_sem.at[kind, p]
        )

    gate_load = pltpu.make_async_copy(gates_hbm, gates_ref, gates_sem.at[0])
    beta_load = pltpu.make_async_copy(betas_hbm, betas_ref, gates_sem.at[1])
    query_load = pltpu.make_async_copy(aq_hbm, aq_ref, query_sem.at[0])

    def of_unit(u, action):
        h = u // 2
        for args in both:
            @pl.when(lax.rem(u, 2) == args[0])
            def _():
                action(h, *args)

    def send_far(u):
        @pl.when((u < units) & (me + 2 < contexts))
        def _():
            of_unit(u, lambda *args: far_copy(*args).start())

    def send_near(u):
        @pl.when((u < units) & even)
        def _():
            of_unit(u, lambda *args: near_copy(*args).start())

    def send_on(u):
        def action(*args):
            far_copy(*args).wait_recv()
            forward_copy(*args).start()

        @pl.when((u < units - 2) & odd & (me >= 3))
        def _():
            of_unit(u, action)

    def issued(k, ahead):
        early = 3 * steps
        count = (jnp.minimum(k, early) * RATE) // 6 + jnp.maximum(k - early, 0) + ahead
        return jnp.minimum(count, units)

    def advance(k, send, ahead):
        done = jnp.where(k == 0, 0, issued(jnp.maximum(k - 1, 0), ahead))
        lax.fori_loop(done, issued(k, ahead), lambda u, c: (send(u), c)[1], 0)

    def issue_free(k):
        @pl.when(even)
        def _():
            advance(k, send_far, FAR_AHEAD)

        @pl.when(k == 1)
        def _():
            advance(0, send_on, PASS_AHEAD)

        advance(k, send_on, PASS_AHEAD)

        @pl.when((k == STAGE_AT) & hops)
        def _():
            for args in both:
                stage_copy(*args).wait_recv()
                hop_copy(*args).start()

    def issue_tight(k):
        @pl.when(odd)
        def _():
            advance(k, send_far, FAR_AHEAD)

        advance(k, send_near, NEAR_AHEAD)

    def issue(k):
        issue_tight(k)
        issue_free(k)

    gate_load.start()
    beta_load.start()
    for args in inputs:
        delta_load(0, *args).start()

    barrier = pltpu.get_barrier_semaphore()
    for by in (-2, -1, 1, 2):
        @pl.when((me + by >= 0) & (me + by < contexts))
        def _():
            pl.semaphore_signal(
                barrier, inc=1, device_id={"ctx": me + by}, device_id_type=pl.DeviceIdType.MESH
            )
    for by in range(1, groups):
        pl.semaphore_signal(
            barrier, inc=1, device_id={"head": lax.rem(group + by, groups)},
            device_id_type=pl.DeviceIdType.MESH,
        )

    def start_delta(p, carry):
        for args in inputs:
            delta_load(p, *args).start()
        return carry

    lax.fori_loop(1, steps, start_delta, 0)

    near_peers = jnp.minimum(me, 2) + jnp.minimum(contexts - 1 - me, 2)
    pl.semaphore_wait(barrier, near_peers + (groups - 1))

    @pl.when(stages)
    def _():
        for args in both:
            stage_copy(*args).start()

    advance(0, send_far, FAR_AHEAD)
    advance(0, send_near, NEAR_AHEAD)
    query_load.start()
    gain_loads = (
        pltpu.make_async_copy(again_hbm, again_ref, gain_sem.at[0]),
        pltpu.make_async_copy(dgain_hbm, dgain_ref, gain_sem.at[1]),
    )
    for load in gain_loads:
        load.start()

    def start_own(h, carry):
        for args in both:
            own_copy(h, *args).start()
        return carry

    lax.fori_loop(0, heads, start_own, 0)

    @pl.when(me < 2)
    def _():
        def clear(h, carry):
            keys[h, far_rows] = jnp.zeros((rows, DH), bf16)
            vals[h, far_rows] = jnp.zeros((rows, DH), bf16)
            return carry
        lax.fori_loop(0, heads, clear, 0)

    @pl.when(me < 1)
    def _():
        def clear(h, carry):
            keys[h, near_rows] = jnp.zeros((rows, DH), bf16)
            vals[h, near_rows] = jnp.zeros((rows, DH), bf16)
            entering[h] = jnp.zeros((DH, DH), bf16)
            return carry
        lax.fori_loop(0, heads, clear, 0)

    gate_load.wait()
    beta_load.wait()
    for h in range(heads):
        gate_ref[h] = gates_ref[h : h + 1]
        beta_ref[h] = betas_ref[h : h + 1]
    attn_sq[...] = jnp.zeros_like(attn_sq)
    delta_sq[...] = jnp.zeros_like(delta_sq)

    scale = math.log2(math.e) / math.sqrt(DH)
    ri = lax.broadcasted_iota(jnp.int32, (QROWS, QROWS), 0)
    ci = lax.broadcasted_iota(jnp.int32, (QROWS, QROWS), 1)
    tiles = WINDOW // QROWS + 1
    first_tile = jnp.maximum(WINDOW - me * rows, 0) // QROWS

    def attend(h, b):
        q_rows = pl.ds(pl.multiple_of(b * QROWS, QROWS), QROWS)
        q = aq_ref[q_rows, lanes(h)]
        scores = []
        for n in range(tiles):
            at = pl.ds(pl.multiple_of((b + n) * QROWS, QROWS), QROWS)
            s = dot(q, keys[h, at], ((1,), (1,))) * scale
            if n < tiles - 1:
                s = s + jnp.where(b + n >= first_tile, 0.0, -1e30).astype(f32)
            if n == 0:
                s = jnp.where(ci > ri, s, -1e30)
            if n == tiles - 1:
                s = jnp.where(ci <= ri, s, -1e30)
            scores.append(s)
        top = jnp.max(functools.reduce(jnp.maximum, scores), axis=1, keepdims=True)
        raised = [jnp.exp2(s - top) for s in scores]
        total = jnp.sum(functools.reduce(jnp.add, raised), axis=1, keepdims=True)
        inverse = 1.0 / total
        out = None
        for n in range(tiles):
            at = pl.ds(pl.multiple_of((b + n) * QROWS, QROWS), QROWS)
            part = dot((raised[n] * inverse).astype(bf16), vals[h, at])
            out = part if out is None else out + part
        attn_out[h, q_rows] = out
        attn_sq[q_rows, :] += out * out

    def relay(p):
        @pl.when(me >= 1)
        def _():
            relay_copy(p).wait_recv()

        @pl.when(me + 1 < contexts)
        def _():
            for e in range(HEADS_STEP):
                h = p * HEADS_STEP + e
                high, low = split(linear[h])
                state = entering[h]
                leaving[h] = (dot(high, state) + dot(low, state) + offset[h]).astype(bf16)
            relay_copy(p).start()

        for e in range(HEADS_STEP):
            h = p * HEADS_STEP + e
            full = delta_out[h] + dot(qeff[h], entering[h])
            delta_out[h] = full
            delta_sq[...] += full * full

    def service(t):
        over = t - 2 * steps
        late = over >= 0
        turn = jnp.where(late, 2 * steps + over // LATE_STRIDE, t)
        q = turn - me

        @pl.when(
            (q >= 0) & (lax.rem(q + 2 * contexts, 2) == 0) & (q < 2 * steps)
            & (jnp.logical_not(late) | (lax.rem(over + 2 * steps * LATE_STRIDE, LATE_STRIDE) == 0))
        )
        def _():
            relay(q // 2)

    def step(s, carry):
        early = s < steps
        mark = jnp.where(early, 3 * s, 3 * steps + 2 * (s - steps))

        @pl.when(early)
        def _():
            for args in inputs:
                delta_load(s, *args).wait()

            issue(mark + 1)
            delta_heads(
                s * HEADS_STEP, lambda: issue(mark + 2), dq_ref, dk_ref, dv_ref, gate_ref, beta_ref,
                delta_out, qeff, linear, offset,
            )

        @pl.when(jnp.logical_not(early))
        def _():
            issue_free(mark + 1)

        service(2 * s)

        @pl.when(jnp.logical_not(early))
        def _():
            issue_tight(mark + 1)

        h = s - ATTEND_LAG

        @pl.when((h >= 0) & (h < heads))
        def _():
            @pl.when(h == 0)
            def _():
                query_load.wait()

            for args in both:
                own_copy(h, *args).wait()

                @pl.when((me >= 2) & jnp.logical_not(odd & (me >= 3) & (h < heads - 1)))
                def _():
                    far_copy(h, *args).wait_recv()

                @pl.when(me >= 1)
                def _():
                    near_copy(h, *args).wait_recv()

            attend(h, 0)

        third = mark + jnp.where(early, 3, 2)
        issue_free(third)
        service(2 * s + 1)
        issue_tight(third)

        @pl.when((h >= 0) & (h < heads))
        def _():
            lax.fori_loop(1, halves, lambda b, c: (attend(h, b), c)[1], 0)

        return carry

    last_turn = max(2 * (steps - 1) + contexts - 1 - 2 * steps, 0)
    turns = max(heads + ATTEND_LAG, steps + heads, steps + (last_turn * LATE_STRIDE) // 2 + 1)
    lax.fori_loop(0, turns, step, 0)
    for load in gain_loads:
        load.wait()

    dr = lax.broadcasted_iota(jnp.int32, (CHUNK, CHUNK), 0)
    dc = lax.broadcasted_iota(jnp.int32, (CHUNK, CHUNK), 1)
    eye = dr == dc
    lines = []
    for part in (attn_sq, delta_sq):
        for b in range(blocks):
            col = jnp.sum(part[b * CHUNK : (b + 1) * CHUNK, :], axis=1, keepdims=True)
            lines.append(jnp.sum(jnp.where(eye, col, 0.0), axis=0, keepdims=True))
    mine = jnp.concatenate(lines, axis=0)
    sums_send[...] = mine

    def sums_copy(by):
        return pltpu.make_async_remote_copy(
            src_ref=sums_send,
            dst_ref=sums_recv.at[by],
            send_sem=sums_ss.at[by],
            recv_sem=sums_rs.at[by],
            device_id={"head": lax.rem(group + by, groups)},
            device_id_type=pl.DeviceIdType.MESH,
        )

    for by in range(1, groups):
        sums_copy(by).start()
    for h in range(heads):
        cs = slice(h * DH, (h + 1) * DH)
        attn_out[h] = again_ref[cs][None, :] * attn_out[h]
        delta_out[h] = dgain_ref[cs][None, :] * delta_out[h]
    whole = mine
    for by in range(1, groups):
        sums_copy(by).wait_recv()
        whole = whole + sums_recv[by]
    scales = lax.rsqrt(whole / (width * groups) + epsilon) * 0.5

    for b in range(blocks):
        rs = slice(b * CHUNK, (b + 1) * CHUNK)
        sa = jnp.sum(jnp.where(eye, scales[b : b + 1], 0.0), axis=1, keepdims=True)
        sd = jnp.sum(
            jnp.where(eye, scales[blocks + b : blocks + b + 1], 0.0), axis=1, keepdims=True
        )
        for h in range(heads):
            cs = slice(h * DH, (h + 1) * DH)
            mixed_ref[rs, cs] = (
                attn_out[h, rs] * sa + delta_out[h, rs] * sd
            ).astype(bf16)

    for by in range(1, groups):
        sums_copy(by).wait_send()

    def drain(h, carry):
        for args in both:
            @pl.when(me + 2 < contexts)
            def _():
                far_copy(h, *args).wait_send()

            @pl.when(even)
            def _():
                near_copy(h, *args).wait_send()

            @pl.when(odd & (me >= 3) & (h < heads - 1))
            def _():
                forward_copy(h, *args).wait_send()

            @pl.when((h == 0) & stages)
            def _():
                stage_copy(*args).wait_send()

            @pl.when((h == 0) & hops)
            def _():
                hop_copy(*args).wait_send()

        return carry

    lax.fori_loop(0, heads, drain, 0)

    @pl.when(me + 1 < contexts)
    def _():
        lax.fori_loop(0, steps, lambda p, c: (relay_copy(p).wait_send(), c)[1], 0)


def on_device(
    attn_query,
    attn_key,
    attn_value,
    delta_query,
    delta_key,
    delta_value,
    delta_gate,
    delta_beta,
    attn_gain,
    delta_gain,
):
    rows, width = attn_query.shape
    heads = width // DH
    groups = lax.axis_size("head")
    lines = 2 * rows // CHUNK
    hbm = pl.BlockSpec(memory_space=pltpu.HBM)
    dma = pltpu.SemaphoreType.DMA
    return pl.pallas_call(
        functools.partial(layer_kernel, contexts=lax.axis_size("ctx"), groups=groups),
        in_specs=[hbm] * 10,
        out_specs=pl.BlockSpec(memory_space=pltpu.VMEM),
        out_shape=pltpu.VMEM((rows, width), bf16),
        scratch_shapes=[
            pltpu.VMEM((rows, width), bf16),
            pltpu.VMEM((rows, width), bf16),
            pltpu.VMEM((rows, width), bf16),
            pltpu.VMEM((rows, width), bf16),
            pltpu.VMEM((heads, rows), f32),
            pltpu.VMEM((heads, rows), f32),
            pltpu.VMEM((heads, WINDOW + rows, DH), bf16),
            pltpu.VMEM((heads, WINDOW + rows, DH), bf16),
            pltpu.VMEM((heads, rows, DH), f32),
            pltpu.VMEM((heads, rows, DH), f32),
            pltpu.VMEM((heads, rows, DH), bf16),
            pltpu.VMEM((heads, DH, DH), f32),
            pltpu.VMEM((heads, DH, DH), f32),
            pltpu.VMEM((heads, DH, DH), bf16),
            pltpu.VMEM((heads, DH, DH), bf16),
            pltpu.VMEM((rows, DH), f32),
            pltpu.VMEM((rows, DH), f32),
            pltpu.VMEM((lines, CHUNK), f32),
            pltpu.VMEM((groups, lines, CHUNK), f32),
            pltpu.VMEM((heads, 1, rows), f32),
            pltpu.VMEM((heads, 1, rows), f32),
            pltpu.VMEM((width,), f32),
            pltpu.VMEM((width,), f32),
            dma((2,)),
            dma((2, heads)),
            dma((2, heads)),
            dma((2, heads)),
            dma((2, heads)),
            dma((2, heads)),
            dma((heads // HEADS_STEP,)),
            dma((heads // HEADS_STEP,)),
            dma((groups,)),
            dma((groups,)),
            dma((1,)),
            dma((2,)),
            dma((3, heads // HEADS_STEP)),
            pltpu.VMEM((2, rows, DH), bf16),
            dma((2,)),
            dma((2,)),
            dma((2,)),
        ],
        compiler_params=pltpu.CompilerParams(
            collective_id=0, has_side_effects=True, vmem_limit_bytes=67043328 - 2 * rows * width - 16384
        ),
        name="layer",
    )(
        attn_query,
        attn_key,
        attn_value,
        delta_query,
        delta_key,
        delta_value,
        delta_gate.T,
        delta_beta.T,
        attn_gain,
        delta_gain,
    )


def solution(mesh):
    both = P("ctx", "head")
    return jax.shard_map(
        on_device,
        mesh=mesh,
        in_specs=(both,) * 8 + (P("head"),) * 2,
        out_specs=both,
        check_vma=False,
    )
```
